256 devices in a mesh: blk: 64 (over y_hi, x, z), dp: 4 (over y_lo, core).
Axes of the slice: x: 4, y: 4 (y_hi: 2, y_lo: 2; y = y_hi * 2 + y_lo), z: 8, core: 2. Of those that a mesh axis runs over, the one named last changes fastest.
Arguments:
- x_rows: bfloat16 [65536, 2048], P('blk'), may hold values from -6 to 6
- grad_rows: bfloat16 [65536, 2048], P('blk'), may hold values from -3 to 3
- w_gate_up: bfloat16 [64, 2, 768, 2048], P('blk', None, 'dp'), may hold values from -0.125 to 0.125
- w_down: bfloat16 [64, 768, 2048], P('blk', 'dp'), may hold values from -0.21875 to 0.21875
- counts: int32 [64, 5], replicated, may hold values from 1 to 384, as said below
Outputs:
- grad_gate_up: float32 [64, 2, 768, 2048], P('blk', None, 'dp')
- grad_down: float32 [64, 768, 2048], P('blk', 'dp')
- grad_x: bfloat16 [65536, 2048], P('blk', 'dp')
The draws below stay inside these ranges and needn't reach their ends.
Inputs may be any that keep to these rules, and one draw needn't show every extreme that they name: `counts`: on every device the 5 offsets take 3, 2, 1, 1 and 1 blocks of 128 rows, in an order drawn for each device, so the blocks fill all 1024 rows; an offset with k blocks has more than 128 * (k - 1) live rows; in every draw some device has an offset with exactly 384 live rows.
All inputs are finite; a program needn't handle non-finite values.
Results may differ from the reference program's by a relative error of at most 0.0095.
Values may be sent and summed in bfloat16 or wider, within the bound.
A program may use at most 192 MiB of HBM per device.

```python
import jax
import jax.numpy as jnp
from jax import lax

D = 2048
FW = 768
BLOCK = 128
SPAN = 5
ROWS_DEV = 1024
EXPERTS = 64
N_BLK = 64
N_DP = 4


def draw_counts(key, part):
    subkeys = jax.random.split(jax.random.fold_in(key, 17), 3)
    orders = jax.vmap(lambda single: jax.random.permutation(single, SPAN))(jax.random.split(subkeys[0], N_BLK))
    rank_table = jnp.argsort(orders, axis=1, stable=True).astype(jnp.int32)
    block_table = jnp.array([3, 2] + [1] * (SPAN - 2), dtype=jnp.int32)
    blocks = block_table[rank_table]
    extra = jax.random.randint(subkeys[1], (N_BLK, SPAN), 0, BLOCK, dtype=jnp.int32)
    result = (blocks - 1) * BLOCK + 1 + extra
    chosen = jax.random.randint(subkeys[2], (), 0, N_BLK, dtype=jnp.int32)
    row_ids = jnp.arange(N_BLK, dtype=jnp.int32)[:, None]
    result = jnp.where((row_ids == chosen) & (blocks == 3), 3 * BLOCK, result)
    return result.astype(jnp.int32)


def level_of(stream_key, extent, pieces, smallest, largest):
    gain, own = 1.0, jax.random.fold_in(stream_key, 6)
    for position, parts in pieces:
        heights = jnp.exp(jax.random.uniform(jax.random.fold_in(own, position), (parts,), jnp.float32, smallest / len(pieces), largest / len(pieces)))
        gain = gain * jnp.repeat(heights, extent[position] // parts).reshape([-1 if axis == position else 1 for axis in range(len(extent))])
    return gain


def noise(own_key, dims, width, limit, shards=(), kind=jnp.bfloat16):
    values = width * jax.random.normal(own_key, dims, jnp.float32)
    if shards:
        values = values * level_of(own_key, dims, shards, -0.22, 0.18)
    return jnp.clip(values, -limit, limit).astype(kind)


def setup_inputs(seed: int = 0) -> dict:
    key_list = jax.random.split(jax.random.key(seed), 6)
    x_rows = noise(key_list[0], (N_BLK * ROWS_DEV, D), 1.0, 6.0, ((0, 64),))
    grad_rows = noise(key_list[1], (N_BLK * ROWS_DEV, D), 0.5, 3.0, ((0, 64),))
    w_gate_up = noise(key_list[2], (EXPERTS, 2, FW, D), D ** -0.5, 0.125, ((0, 64), (2, 4)))
    w_down = noise(key_list[3], (EXPERTS, FW, D), FW ** -0.5, 0.21875, ((0, 64), (1, 4)))
    counts = draw_counts(jax.random.fold_in(key_list[5], 71), 0)
    return dict(x_rows=x_rows, grad_rows=grad_rows, w_gate_up=w_gate_up, w_down=w_down, counts=counts)


def contract_last(lhs_array, rhs_array):
    return lax.dot_general(lhs_array, rhs_array, (((1,), (1,)), ((), ())), preferred_element_type=jnp.float32)


def contract_first(lhs_array, rhs_array):
    return lax.dot_general(lhs_array, rhs_array, (((0,), (0,)), ((), ())), preferred_element_type=jnp.float32)


def block_grads(weight_in, weight_out, rows_in, rows_cot):
    unit_count = weight_out.shape[0]
    projected = contract_last(rows_in, weight_in.reshape(2 * unit_count, weight_in.shape[2]))
    gate_pre = projected[:, :unit_count]
    up_pre = projected[:, unit_count:]
    sigmoid_gate = jax.nn.sigmoid(gate_pre)
    active = gate_pre * sigmoid_gate
    hidden = (active * up_pre).astype(jnp.bfloat16)
    hidden_grad = contract_last(rows_cot, weight_out)
    gate_gradient_rows = (hidden_grad * up_pre * sigmoid_gate * (1.0 + gate_pre * (1.0 - sigmoid_gate))).astype(jnp.bfloat16)
    up_gradient_rows = (hidden_grad * active).astype(jnp.bfloat16)
    grad_in = jnp.stack([contract_first(gate_gradient_rows, rows_in), contract_first(up_gradient_rows, rows_in)])
    grad_out = contract_first(hidden, rows_cot)
    row_grand_count = rows_in.shape[0]
    fourth_portion = unit_count // N_DP
    partial_value_sum = jnp.einsum("ewi,wip->ewp", gate_gradient_rows.reshape(row_grand_count, N_DP, fourth_portion).astype(jnp.float32),
                         weight_in[0].reshape(N_DP, fourth_portion, -1).astype(jnp.float32), precision=lax.Precision.HIGHEST)
    partial_value_sum = partial_value_sum + jnp.einsum("ewi,wip->ewp", up_gradient_rows.reshape(row_grand_count, N_DP, fourth_portion).astype(jnp.float32),
                                   weight_in[1].reshape(N_DP, fourth_portion, -1).astype(jnp.float32), precision=lax.Precision.HIGHEST)
    return grad_in, grad_out, partial_value_sum


def reference(x_rows, grad_rows, w_gate_up, w_down, counts):
    inputs_all = x_rows.reshape(N_BLK, ROWS_DEV, D)
    cotan_all = grad_rows.reshape(N_BLK, ROWS_DEV, D)

    def device_step(totals, packed):
        device, inputs, cotangent = packed
        own_counts = lax.dynamic_index_in_dim(counts, device, 0, keepdims=False).astype(jnp.int32)
        blocks = ((own_counts + BLOCK - 1) // BLOCK).astype(jnp.int32)
        block_limits = jnp.cumsum(blocks).astype(jnp.int32)
        starts = ((block_limits - blocks) * BLOCK).astype(jnp.int32)

        def block_step(running, block_idx):
            acc_in, acc_out = running
            offset = jnp.minimum(jnp.sum((block_limits <= block_idx).astype(jnp.int32)).astype(jnp.int32), SPAN - 1)
            row_first = (block_idx * BLOCK).astype(jnp.int32)
            local_row = row_first - starts[offset] + jnp.arange(BLOCK, dtype=jnp.int32)
            live_rows = local_row < own_counts[offset]
            rows_in = lax.dynamic_slice_in_dim(inputs, row_first, BLOCK, 0)
            rows_cot = lax.dynamic_slice_in_dim(cotangent, row_first, BLOCK, 0)
            rows_cot = jnp.where(live_rows[:, None], rows_cot, jnp.zeros((), rows_cot.dtype))
            expert = ((device - offset) % N_BLK).astype(jnp.int32)
            weight_in = lax.dynamic_index_in_dim(w_gate_up, expert, 0, keepdims=False)
            weight_out = lax.dynamic_index_in_dim(w_down, expert, 0, keepdims=False)
            grad_in, grad_out, partial_value_sum = block_grads(weight_in, weight_out, rows_in, rows_cot)
            acc_in = acc_in.at[expert].add(grad_in)
            acc_out = acc_out.at[expert].add(grad_out)
            return (acc_in, acc_out), partial_value_sum

        totals, partial_value_sum = lax.scan(block_step, totals, jnp.arange(ROWS_DEV // BLOCK, dtype=jnp.int32))
        partial_value_sum = partial_value_sum.reshape(ROWS_DEV, N_DP, D)
        rounded = lax.optimization_barrier(partial_value_sum.astype(jnp.bfloat16))
        result = jnp.sum(rounded.astype(jnp.float32), axis=1).astype(jnp.bfloat16)
        return totals, result

    start_in = jnp.zeros(w_gate_up.shape, jnp.float32)
    start_out = jnp.zeros(w_down.shape, jnp.float32)
    (grad_gate_up, grad_down), result = lax.scan(
        device_step, (start_in, start_out), (jnp.arange(N_BLK, dtype=jnp.int32), inputs_all, cotan_all))
    return grad_gate_up, grad_down, result.reshape(N_BLK * ROWS_DEV, D)
```

```python
import jax
import jax.numpy as jnp
from jax import lax
from jax.experimental import pallas as pl
from jax.experimental.pallas import tpu as pltpu
from jax.sharding import Mesh
from jax.sharding import PartitionSpec as P

HOPS = 4
BLOCK = 128
SLOTS = 3
DP = ("dp_0", "dp_1")
MESH = pl.DeviceIdType.MESH
UNITS = SLOTS * (HOPS + 1)
REMOTE = SLOTS * HOPS


def contract_last(lhs, rhs):
    return lax.dot_general(lhs, rhs, (((1,), (1,)), ((), ())), preferred_element_type=jnp.float32)


def contract_first(lhs, rhs):
    return lax.dot_general(lhs, rhs, (((0,), (0,)), ((), ())), preferred_element_type=jnp.float32)


def kernel(
    n_blk,
    counts,
    x_hbm,
    g_hbm,
    w_in,
    w_out,
    grad_in,
    grad_out,
    grad_x,
    x_quarter,
    g_quarter,
    staged,
    full,
    pieces,
    pieces_in,
    half_out,
    half_in,
    home_out,
    home,
    load_sem,
    z_send,
    z_recv,
    y_send,
    y_recv,
    c_send,
    c_recv,
    d_send,
    d_recv,
    p_send,
    p_recv,
    h_send,
    h_recv,
    r_send,
    r_recv,
):
    b, y, c = lax.axis_index("blk"), lax.axis_index("dp_0"), lax.axis_index("dp_1")
    unit_count = w_out.shape[0]
    quarter = x_quarter.shape[2]

    def around(steps):
        return lax.rem(b + steps + n_blk, n_blk)

    y_peer, c_peer = (b, 1 - y, c), (b, y, 1 - c)

    def cols(y_of, c_of):
        return pl.ds(pl.multiple_of((2 * y_of + c_of) * quarter, quarter), quarter)

    own = cols(y, c)
    loads = [
        pltpu.make_async_copy(x_hbm.at[:, :, own], x_quarter, load_sem.at[0]),
        pltpu.make_async_copy(g_hbm.at[:, :, own], g_quarter, load_sem.at[1]),
    ]
    for k in range(SLOTS):
        loads.append(pltpu.make_async_copy(x_hbm.at[k], full.at[k, 0], load_sem.at[2 + 2 * k]))
        loads.append(pltpu.make_async_copy(g_hbm.at[k], full.at[k, 1], load_sem.at[3 + 2 * k]))
    for load in loads:
        load.start()

    barrier = pltpu.get_barrier_semaphore()
    for o in range(1, HOPS + 1):
        for steps in (o, -o):
            pl.semaphore_signal(barrier, 1, device_id=(around(steps), y, c), device_id_type=MESH)
    pl.semaphore_signal(barrier, 1, device_id=y_peer, device_id_type=MESH)
    pl.semaphore_signal(barrier, 1, device_id=c_peer, device_id_type=MESH)

    live_of = [counts[b, o] for o in range(HOPS + 1)]
    blocks = [lax.shift_right_logical(n + (BLOCK - 1), 7) for n in live_of]
    starts = [jnp.int32(0)]
    for o in range(HOPS):
        starts.append(starts[o] + blocks[o])
    row_id = lax.broadcasted_iota(jnp.int32, (BLOCK, 1), 0)

    def remote(src, dst, send, recv, target):
        return pltpu.make_async_remote_copy(
            src_ref=src, dst_ref=dst, send_sem=send, recv_sem=recv, device_id=target, device_id_type=MESH
        )

    def z_copy(j, o):
        return remote(
            staged.at[j],
            full.at[SLOTS + j, :, :, own],
            z_send.at[j],
            z_recv.at[j],
            (around(-o), y, c),
        )

    loads[0].wait()
    loads[1].wait()
    pl.semaphore_wait(barrier, 2 * HOPS + 2)
    for j in range(REMOTE):
        k, o = j // HOPS, 1 + j % HOPS
        block = jnp.clip(starts[o] + jnp.minimum(k, blocks[o] - 1), 0, x_quarter.shape[0] - 1)
        staged[j, 0] = x_quarter[block]
        live = row_id < live_of[o] - k * BLOCK
        staged[j, 1] = jnp.where(live, g_quarter[block], jnp.zeros((), jnp.bfloat16))
        z_copy(j, o).start()

    for load in loads[2:]:
        load.wait()
    for k in range(SLOTS):
        live = row_id < live_of[0] - k * BLOCK
        full[k, 1] = jnp.where(live, full[k, 1], jnp.zeros((), jnp.bfloat16))
    grad_in[...] = jnp.zeros_like(grad_in)
    grad_out[...] = jnp.zeros_like(grad_out)

    def y_copy(j):
        part = full.at[SLOTS + j, :, :, own]
        return remote(part, part, y_send.at[j], y_recv.at[j], y_peer)

    def c_copy(j):
        part = full.at[SLOTS + j, :, :, own]
        return remote(part, part, c_send.at[j], c_recv.at[j], c_peer)

    def d_copy(j):
        part = full.at[SLOTS + j, :, :, cols(1 - y, c)]
        return remote(part, part, d_send.at[j], d_recv.at[j], c_peer)

    def p_copy(u):
        return remote(pieces.at[u, 1 - c], pieces_in.at[u], p_send.at[u], p_recv.at[u], c_peer)

    def h_copy(u):
        return remote(half_out.at[u], half_in.at[u], h_send.at[u], h_recv.at[u], y_peer)

    def r_copy(j):
        o = 1 + lax.rem(j, HOPS)
        return remote(home_out.at[j], home.at[SLOTS + j], r_send.at[j], r_recv.at[j], (around(o), y, c))

    def compute(u):
        rows_in, rows_cot = full[u, 0], full[u, 1]
        projected = contract_last(rows_in, w_in[...])
        gate_pre, up_pre = projected[:, :unit_count], projected[:, unit_count:]
        sigmoid_gate = jax.nn.sigmoid(gate_pre)
        active = gate_pre * sigmoid_gate
        hidden = (active * up_pre).astype(jnp.bfloat16)
        hidden_grad = contract_last(rows_cot, w_out[...])
        gate_grad = hidden_grad * up_pre * sigmoid_gate * (1.0 + gate_pre * (1.0 - sigmoid_gate))
        both = jnp.concatenate([gate_grad, hidden_grad * active], axis=1).astype(jnp.bfloat16)
        for q in range(4):
            pieces[u, q % 2, q // 2] = jnp.dot(
                both, w_in[:, q * quarter : (q + 1) * quarter], preferred_element_type=jnp.float32
            ).astype(jnp.bfloat16)
        p_copy(u).start()
        grad_in[...] += contract_first(both, rows_in)
        grad_out[...] += contract_first(hidden, rows_cot)

    def partial_sum(u, y_of):
        return pieces[u, c, y_of].astype(jnp.float32) + pieces_in[u, y_of].astype(jnp.float32)

    def step(s, carry):
        @pl.when((s >= 2) & (s < UNITS + 2))
        def _():
            u = s - 2

            @pl.when(u >= SLOTS)
            def _():
                c_copy(u - SLOTS).wait_recv()
                d_copy(u - SLOTS).wait_recv()

            compute(u)

        @pl.when((s >= 3) & (s < UNITS + 3))
        def _():
            u = s - 3
            p_copy(u).wait_recv()
            half_out[u] = partial_sum(u, 1 - y).astype(jnp.bfloat16)
            h_copy(u).start()

        @pl.when((s >= 4) & (s < UNITS + 4))
        def _():
            u = s - 4
            h_copy(u).wait_recv()
            total = (partial_sum(u, y) + half_in[u].astype(jnp.float32)).astype(jnp.bfloat16)

            @pl.when(u < SLOTS)
            def _():
                home[u] = total

            @pl.when(u >= SLOTS)
            def _():
                home_out[u - SLOTS] = total
                r_copy(u - SLOTS).start()

        @pl.when((s >= 1 + SLOTS) & (s < UNITS + 1))
        def _():
            j = s - 1 - SLOTS
            y_copy(j).wait_recv()
            d_copy(j).start()

        @pl.when((s >= SLOTS) & (s < UNITS))
        def _():
            j = s - SLOTS
            z_copy(j, 1).wait_recv()
            y_copy(j).start()
            c_copy(j).start()

        return carry

    lax.fori_loop(0, UNITS + 4, step, 0)

    def drain(j, carry):
        r_copy(j).wait_recv()
        z_copy(j, 1).wait_send()
        y_copy(j).wait_send()
        c_copy(j).wait_send()
        d_copy(j).wait_send()
        r_copy(j).wait_send()
        return carry

    lax.fori_loop(0, REMOTE, drain, 0)

    def drain_sums(u, carry):
        p_copy(u).wait_send()
        h_copy(u).wait_send()
        return carry

    lax.fori_loop(0, UNITS, drain_sums, 0)

    for p in range(grad_x.shape[0] // BLOCK):
        unit = jnp.int32(0)
        for o in range(HOPS + 1):
            k = p - starts[o]
            here = k if o == 0 else SLOTS + k * HOPS + o - 1
            unit = jnp.where((k >= 0) & (k < blocks[o]), here, unit)
        grad_x[pl.ds(p * BLOCK, BLOCK), :] = home[jnp.clip(unit, 0, UNITS - 1)]


def on_device(x_rows, grad_rows, w_gate_up, w_down, counts):
    rows, features = x_rows.shape
    units = w_down.shape[1]
    quarter = features // 4
    vmem = pl.BlockSpec(memory_space=pltpu.VMEM)
    held = pl.BlockSpec(memory_space=pl.ANY)
    b16, f32 = jnp.bfloat16, jnp.float32
    dma = pltpu.SemaphoreType.DMA
    grad_in, grad_out, grad_x = pl.pallas_call(
        lambda *refs: kernel(lax.axis_size("blk"), *refs),
        name="experts_backward",
        out_shape=(
            jax.ShapeDtypeStruct((2 * units, features), f32),
            jax.ShapeDtypeStruct((units, features), f32),
            jax.ShapeDtypeStruct((rows, quarter), b16),
        ),
        in_specs=[pl.BlockSpec(memory_space=pltpu.SMEM), held, held, vmem, vmem],
        out_specs=(vmem, vmem, vmem),
        scratch_shapes=[
            pltpu.VMEM((rows // BLOCK, BLOCK, quarter), b16),
            pltpu.VMEM((rows // BLOCK, BLOCK, quarter), b16),
            pltpu.VMEM((REMOTE, 2, BLOCK, quarter), b16),
            pltpu.VMEM((UNITS, 2, BLOCK, features), b16),
            pltpu.VMEM((UNITS, 2, 2, BLOCK, quarter), b16),
            pltpu.VMEM((UNITS, 2, BLOCK, quarter), b16),
            pltpu.VMEM((UNITS, BLOCK, quarter), b16),
            pltpu.VMEM((UNITS, BLOCK, quarter), b16),
            pltpu.VMEM((REMOTE, BLOCK, quarter), b16),
            pltpu.VMEM((UNITS, BLOCK, quarter), b16),
            dma((2 + 2 * SLOTS,)),
            *[dma((REMOTE,))] * 8,
            *[dma((UNITS,))] * 4,
            *[dma((REMOTE,))] * 2,
        ],
        compiler_params=pltpu.CompilerParams(
            collective_id=0, has_side_effects=True, vmem_limit_bytes=60 * 1024 * 1024
        ),
    )(
        counts,
        x_rows.reshape(-1, BLOCK, features),
        grad_rows.reshape(-1, BLOCK, features),
        w_gate_up.reshape(2 * units, features),
        w_down.reshape(units, features),
    )
    return (grad_in.reshape(1, 2, units, features), grad_out[None], grad_x)


def solution(mesh):
    finer = Mesh(mesh.devices.reshape(mesh.shape["blk"], 2, 2), ("blk", "dp_0", "dp_1"))
    placed = (P("blk", None), P("blk", None), P("blk", None, DP, None), P("blk", DP, None), P())
    return jax.shard_map(
        on_device,
        mesh=finer,
        in_specs=placed,
        out_specs=(P("blk", None, DP, None), P("blk", DP, None), P("blk", DP)),
        check_vma=False,
    )
```

```python
import jax
import jax.numpy as jnp
from jax import lax
from jax.experimental import pallas as pl
from jax.experimental.pallas import tpu as pltpu
from jax.sharding import Mesh
from jax.sharding import PartitionSpec as P

HOPS = 4
BLOCK = 128
SLOTS = 3
DP = ("dp_0", "dp_1")
MESH = pl.DeviceIdType.MESH
UNITS = SLOTS * (HOPS + 1)
REMOTE = SLOTS * HOPS


def contract_last(lhs, rhs):
    return lax.dot_general(lhs, rhs, (((1,), (1,)), ((), ())), preferred_element_type=jnp.float32)


def contract_first(lhs, rhs):
    return lax.dot_general(lhs, rhs, (((0,), (0,)), ((), ())), preferred_element_type=jnp.float32)


HALF_WAY = HOPS
COLUMN = 8
IN_FLIGHT = 4


def offset_of(j):
    turn, i = j // HOPS, j % HOPS
    last = turn // (SLOTS - 1)
    return (1 - last) * (i + 1 + i // 2 - 2 * (i // 3)) + last * (HOPS - i)


UNIT_OF = {(offset_of(j), j // HOPS): j for j in range(REMOTE)}
DIRECT = [j for j in range(REMOTE) if offset_of(j) < HALF_WAY]
RELAYED = [j for j in range(REMOTE) if offset_of(j) == HALF_WAY]


def kernel(
    n_blk,
    counts_hbm,
    x_hbm,
    g_hbm,
    w_in,
    w_out,
    grad_in,
    grad_out,
    grad_x,
    x_quarter,
    g_quarter,
    staged,
    passing,
    full,
    pieces,
    pieces_in,
    half_out,
    half_in,
    home_out,
    home,
    counts,
    load_sem,
    z_send,
    z_recv,
    n_send,
    n_recv,
    y_send,
    y_recv,
    c_send,
    c_recv,
    d_send,
    d_recv,
    p_send,
    p_recv,
    h_send,
    h_recv,
    r_send,
    r_recv,
):
    b, y, c = lax.axis_index("blk"), lax.axis_index("dp_0"), lax.axis_index("dp_1")
    unit_count = w_out.shape[0]
    quarter = x_quarter.shape[2]

    def around(steps):
        return lax.rem(b + steps + n_blk, n_blk)

    def up(position, steps):
        level = lax.rem(position, COLUMN)
        return position - level + lax.rem(level + steps, COLUMN)

    y_peer, c_peer = (b, 1 - y, c), (b, y, 1 - c)
    relay_to = (up(b, 1), y, c)
    passed_to = (lax.rem(up(b, COLUMN - 1) - HALF_WAY + n_blk, n_blk), y, c)

    def cols(y_of, c_of):
        return pl.ds(pl.multiple_of((2 * y_of + c_of) * quarter, quarter), quarter)

    own = cols(y, c)
    loads = [
        pltpu.make_async_copy(x_hbm.at[:, :, own], x_quarter, load_sem.at[0]),
        pltpu.make_async_copy(g_hbm.at[:, :, own], g_quarter, load_sem.at[1]),
    ]
    for k in range(SLOTS):
        loads.append(pltpu.make_async_copy(x_hbm.at[k], full.at[k, 0], load_sem.at[2 + 2 * k]))
        loads.append(pltpu.make_async_copy(g_hbm.at[k], full.at[k, 1], load_sem.at[3 + 2 * k]))
    loads.append(pltpu.make_async_copy(counts_hbm, counts, load_sem.at[2 + 2 * SLOTS]))
    for load in loads:
        load.start()

    barrier = pltpu.get_barrier_semaphore()
    senders = [(around(steps), y, c) for steps in (1, 2, 3, -1, -2, -3, -4)]
    senders += [(up(b, COLUMN - 1), y, c), (up(around(HALF_WAY), 1), y, c), y_peer, c_peer]
    for sender in senders:
        pl.semaphore_signal(barrier, 1, device_id=sender, device_id_type=MESH)

    for load in (loads[0], loads[1], loads[-1]):
        load.wait()
    live_of = [counts[b, o] for o in range(HOPS + 1)]
    blocks = [lax.shift_right_logical(n + (BLOCK - 1), 7) for n in live_of]
    starts = [jnp.int32(0)]
    for o in range(HOPS):
        starts.append(starts[o] + blocks[o])
    row_id = lax.broadcasted_iota(jnp.int32, (BLOCK, 1), 0)

    def remote(src, dst, send, recv, target):
        return pltpu.make_async_remote_copy(
            src_ref=src, dst_ref=dst, send_sem=send, recv_sem=recv, device_id=target, device_id_type=MESH
        )

    def z_copy(j, target):
        return remote(staged.at[j], full.at[SLOTS + j, :, :, own], z_send.at[j], z_recv.at[j], target)

    def start_direct(j):
        z_copy(j, (around(-offset_of(j)), y, c)).start()

    def relay_copy(k):
        j = UNIT_OF[HALF_WAY, k]
        return remote(staged.at[j], passing.at[k], z_send.at[j], n_recv.at[k], relay_to)

    def pass_copy(k):
        j = UNIT_OF[HALF_WAY, k]
        return remote(passing.at[k], full.at[SLOTS + j, :, :, own], n_send.at[k], z_recv.at[j], passed_to)

    for count, j in enumerate(RELAYED[:1] + DIRECT[:1] + RELAYED[1:] + DIRECT[1:]):
        k, o = j // HOPS, offset_of(j)
        block = jnp.clip(starts[o] + jnp.minimum(k, blocks[o] - 1), 0, x_quarter.shape[0] - 1)
        staged[j, 0] = x_quarter[block]
        live = row_id < live_of[o] - k * BLOCK
        staged[j, 1] = jnp.where(live, g_quarter[block], jnp.zeros((), jnp.bfloat16))
        if count == 0:
            pl.semaphore_wait(barrier, len(senders))
        if o == HALF_WAY:
            relay_copy(k).start()
        elif j in DIRECT[:IN_FLIGHT]:
            start_direct(j)

    for load in loads[2:-1]:
        load.wait()
    for k in range(SLOTS):
        live = row_id < live_of[0] - k * BLOCK
        full[k, 1] = jnp.where(live, full[k, 1], jnp.zeros((), jnp.bfloat16))
    grad_in[...] = jnp.zeros_like(grad_in)
    grad_out[...] = jnp.zeros_like(grad_out)

    def y_copy(j):
        part = full.at[SLOTS + j, :, :, own]
        return remote(part, part, y_send.at[j], y_recv.at[j], y_peer)

    def c_copy(j):
        part = full.at[SLOTS + j, :, :, own]
        return remote(part, part, c_send.at[j], c_recv.at[j], c_peer)

    def d_copy(j):
        part = full.at[SLOTS + j, :, :, cols(1 - y, c)]
        return remote(part, part, d_send.at[j], d_recv.at[j], c_peer)

    def p_copy(u):
        return remote(pieces.at[u, 1 - c], pieces_in.at[u], p_send.at[u], p_recv.at[u], c_peer)

    def h_copy(u):
        return remote(half_out.at[u], half_in.at[u], h_send.at[u], h_recv.at[u], y_peer)

    def r_copy(j):
        o = offset_of(j)
        return remote(home_out.at[j], home.at[SLOTS + j], r_send.at[j], r_recv.at[j], (around(o), y, c))

    def compute(u):
        rows_in, rows_cot = full[u, 0], full[u, 1]
        projected = contract_last(rows_in, w_in[...])
        gate_pre, up_pre = projected[:, :unit_count], projected[:, unit_count:]
        sigmoid_gate = jax.nn.sigmoid(gate_pre)
        active = gate_pre * sigmoid_gate
        hidden = (active * up_pre).astype(jnp.bfloat16)
        hidden_grad = contract_last(rows_cot, w_out[...])
        gate_grad = hidden_grad * up_pre * sigmoid_gate * (1.0 + gate_pre * (1.0 - sigmoid_gate))
        both = jnp.concatenate([gate_grad, hidden_grad * active], axis=1).astype(jnp.bfloat16)
        for q in range(4):
            pieces[u, q % 2, q // 2] = jnp.dot(
                both, w_in[:, q * quarter : (q + 1) * quarter], preferred_element_type=jnp.float32
            ).astype(jnp.bfloat16)
        p_copy(u).start()
        grad_in[...] += contract_first(both, rows_in)
        grad_out[...] += contract_first(hidden, rows_cot)

    def partial_sum(u, y_of):
        return pieces[u, c, y_of].astype(jnp.float32) + pieces_in[u, y_of].astype(jnp.float32)

    def step(s, carry):
        for i, j in enumerate(DIRECT[IN_FLIGHT:]):

            @pl.when(s == i + 2)
            def _():
                z_copy(DIRECT[i], y_peer).wait_send()
                start_direct(j)

        @pl.when(s >= 2)
        def _():
            u = s - 2
            h_copy(u).wait_recv()
            total = (partial_sum(u, y) + half_in[u].astype(jnp.float32)).astype(jnp.bfloat16)

            @pl.when(u < SLOTS)
            def _():
                home[u] = total

            @pl.when(u >= SLOTS)
            def _():
                home_out[u - SLOTS] = total
                r_copy(u - SLOTS).start()

        @pl.when((s >= 1) & (s < UNITS + 1))
        def _():
            u = s - 1
            p_copy(u).wait_recv()
            half_out[u] = partial_sum(u, 1 - y).astype(jnp.bfloat16)
            h_copy(u).start()

        @pl.when(s < UNITS)
        def _():
            @pl.when(s >= SLOTS)
            def _():
                c_copy(s - SLOTS).wait_recv()
                d_copy(s - SLOTS).wait_recv()

            compute(s)

        @pl.when((s + 1 >= SLOTS) & (s + 1 < UNITS))
        def _():
            j = s + 1 - SLOTS
            y_copy(j).wait_recv()
            d_copy(j).start()

        for k in range(SLOTS):

            @pl.when(s == k)
            def _():
                relay_copy(k).wait_recv()
                pass_copy(k).start()

        @pl.when((s + 2 >= SLOTS) & (s + 2 < UNITS))
        def _():
            j = s + 2 - SLOTS
            z_copy(j, y_peer).wait_recv()
            y_copy(j).start()
            c_copy(j).start()

        return carry

    lax.fori_loop(0, UNITS + 2, step, 0)

    for j in RELAYED + DIRECT[-IN_FLIGHT:]:
        z_copy(j, y_peer).wait_send()
    for k in range(SLOTS):
        pass_copy(k).wait_send()

    def drain(j, carry):
        r_copy(j).wait_recv()
        y_copy(j).wait_send()
        c_copy(j).wait_send()
        d_copy(j).wait_send()
        r_copy(j).wait_send()
        return carry

    lax.fori_loop(0, REMOTE, drain, 0)

    def drain_sums(u, carry):
        p_copy(u).wait_send()
        h_copy(u).wait_send()
        return carry

    lax.fori_loop(0, UNITS, drain_sums, 0)

    for p in range(grad_x.shape[0] // BLOCK):
        unit = jnp.int32(0)
        for o in range(HOPS + 1):
            for k in range(SLOTS):
                here = k if o == 0 else SLOTS + UNIT_OF[o, k]
                unit = jnp.where((starts[o] + k == p) & (k < blocks[o]), here, unit)
        grad_x[pl.ds(p * BLOCK, BLOCK), :] = home[jnp.clip(unit, 0, UNITS - 1)]


def on_device(x_rows, grad_rows, w_gate_up, w_down, counts):
    rows, features = x_rows.shape
    units = w_down.shape[1]
    quarter = features // 4
    vmem = pl.BlockSpec(memory_space=pltpu.VMEM)
    held = pl.BlockSpec(memory_space=pl.ANY)
    b16, f32 = jnp.bfloat16, jnp.float32
    dma = pltpu.SemaphoreType.DMA
    grad_in, grad_out, grad_x = pl.pallas_call(
        lambda *refs: kernel(lax.axis_size("blk"), *refs),
        name="experts_backward",
        out_shape=(
            jax.ShapeDtypeStruct((2 * units, features), f32),
            jax.ShapeDtypeStruct((units, features), f32),
            jax.ShapeDtypeStruct((rows, quarter), b16),
        ),
        in_specs=[held, held, held, vmem, vmem],
        out_specs=(vmem, vmem, vmem),
        scratch_shapes=[
            pltpu.VMEM((rows // BLOCK, BLOCK, quarter), b16),
            pltpu.VMEM((rows // BLOCK, BLOCK, quarter), b16),
            pltpu.VMEM((REMOTE, 2, BLOCK, quarter), b16),
            pltpu.VMEM((SLOTS, 2, BLOCK, quarter), b16),
            pltpu.VMEM((UNITS, 2, BLOCK, features), b16),
            pltpu.VMEM((UNITS, 2, 2, BLOCK, quarter), b16),
            pltpu.VMEM((UNITS, 2, BLOCK, quarter), b16),
            pltpu.VMEM((UNITS, BLOCK, quarter), b16),
            pltpu.VMEM((UNITS, BLOCK, quarter), b16),
            pltpu.VMEM((REMOTE, BLOCK, quarter), b16),
            pltpu.VMEM((UNITS, BLOCK, quarter), b16),
            pltpu.SMEM(counts.shape, counts.dtype),
            dma((3 + 2 * SLOTS,)),
            *[dma((REMOTE,))] * 2,
            *[dma((SLOTS,))] * 2,
            *[dma((REMOTE,))] * 6,
            *[dma((UNITS,))] * 4,
            *[dma((REMOTE,))] * 2,
        ],
        compiler_params=pltpu.CompilerParams(
            collective_id=0, has_side_effects=True, vmem_limit_bytes=60 * 1024 * 1024
        ),
    )(
        counts,
        x_rows.reshape(-1, BLOCK, features),
        grad_rows.reshape(-1, BLOCK, features),
        w_gate_up.reshape(2 * units, features),
        w_down.reshape(units, features),
    )
    return (grad_in.reshape(1, 2, units, features), grad_out[None], grad_x)


def solution(mesh):
    finer = Mesh(mesh.devices.reshape(mesh.shape["blk"], 2, 2), ("blk", "dp_0", "dp_1"))
    placed = (P("blk", None), P("blk", None), P("blk", None, DP, None), P("blk", DP, None), P())
    return jax.shard_map(
        on_device,
        mesh=finer,
        in_specs=placed,
        out_specs=(P("blk", None, DP, None), P("blk", DP, None), P("blk", DP)),
        check_vma=False,
    )
```

```python
import jax
import jax.numpy as jnp
from jax import lax
from jax.experimental import pallas as pl
from jax.experimental.pallas import tpu as pltpu
from jax.sharding import Mesh
from jax.sharding import PartitionSpec as P

HOPS = 4
BLOCK = 128
SLOTS = 3
DP = ("dp_0", "dp_1")
MESH = pl.DeviceIdType.MESH
UNITS = SLOTS * (HOPS + 1)
REMOTE = SLOTS * HOPS


def contract_last(lhs, rhs):
    return lax.dot_general(lhs, rhs, (((1,), (1,)), ((), ())), preferred_element_type=jnp.float32)


def contract_first(lhs, rhs):
    return lax.dot_general(lhs, rhs, (((0,), (0,)), ((), ())), preferred_element_type=jnp.float32)


HALF_WAY = HOPS
COLUMN = 8
HALF = 32
IN_FLIGHT = 4


def offset_of(j):
    turn, i = j // HOPS, j % HOPS
    last = turn // (SLOTS - 1)
    return (1 - last) * (i + 1 + i // 2 - 2 * (i // 3)) + last * (HOPS - i)


UNIT_OF = {(offset_of(j), j // HOPS): j for j in range(REMOTE)}
DIRECT = [j for j in range(REMOTE) if offset_of(j) < HALF_WAY]
RELAYED = [j for j in range(REMOTE) if offset_of(j) == HALF_WAY]


def kernel(
    n_blk,
    counts_hbm,
    x_hbm,
    g_hbm,
    w_in,
    w_out,
    grad_in,
    grad_out,
    grad_x,
    x_quarter,
    g_quarter,
    staged,
    passing,
    full,
    pieces,
    pieces_in,
    half_out,
    half_in,
    home_out,
    home,
    counts,
    load_sem,
    z_send,
    z_recv,
    n_send,
    n_recv,
    y_send,
    y_recv,
    c_send,
    c_recv,
    d_send,
    d_recv,
    p_send,
    p_recv,
    h_send,
    h_recv,
    r_send,
    r_recv,
):
    b, y, c = lax.axis_index("blk"), lax.axis_index("dp_0"), lax.axis_index("dp_1")
    unit_count = w_out.shape[0]
    quarter = x_quarter.shape[3]

    def up(position, steps):
        level = lax.rem(position, COLUMN)
        return position - level + lax.rem(level + steps, COLUMN)

    def behind(position, o):
        crossed = 1 - (lax.rem(position, HALF) - o + HALF) // HALF
        return (lax.rem(position - o + n_blk, n_blk), y + crossed * (1 - 2 * y), c)

    def ahead(position, o):
        crossed = (lax.rem(position, HALF) + o) // HALF
        return (lax.rem(position + o, n_blk), y + crossed * (1 - 2 * y), c)

    y_peer, c_peer = (b, 1 - y, c), (b, y, 1 - c)
    relay_to = (up(b, 1), y, c)
    passed_to = behind(up(b, COLUMN - 1), HALF_WAY)

    def cols(y_of, c_of):
        return pl.ds(pl.multiple_of((2 * y_of + c_of) * quarter, quarter), quarter)

    own = cols(y, c)
    loads = []
    for y_of in range(2):
        for held, source in ((x_quarter, x_hbm), (g_quarter, g_hbm)):
            copy = pltpu.make_async_copy(source.at[:, :, cols(y_of, c)], held.at[y_of], load_sem.at[len(loads)])
            loads.append(copy)
    for k in range(SLOTS):
        for held, source in ((0, x_hbm), (1, g_hbm)):
            loads.append(pltpu.make_async_copy(source.at[k], full.at[k, held], load_sem.at[len(loads)]))
    loads.append(pltpu.make_async_copy(counts_hbm, counts, load_sem.at[len(loads)]))
    for load in loads:
        load.start()

    barrier = pltpu.get_barrier_semaphore()
    senders = [ahead(b, o) for o in range(1, HALF_WAY)] + [behind(b, o) for o in range(1, HOPS + 1)]
    home_of_far = ahead(b, HALF_WAY)
    senders += [(up(b, COLUMN - 1), y, c), (up(home_of_far[0], 1), home_of_far[1], c), y_peer, c_peer]
    for sender in senders:
        pl.semaphore_signal(barrier, 1, device_id=sender, device_id_type=MESH)

    for load in (*loads[:4], loads[-1]):
        load.wait()
    live_of = [counts[o, b] for o in range(HOPS + 1)]
    blocks = [lax.shift_right_logical(n + (BLOCK - 1), 7) for n in live_of]
    starts = [jnp.int32(0)]
    for o in range(HOPS):
        starts.append(starts[o] + blocks[o])
    row_id = lax.broadcasted_iota(jnp.int32, (BLOCK, 1), 0)

    def remote(src, dst, send, recv, target):
        return pltpu.make_async_remote_copy(
            src_ref=src, dst_ref=dst, send_sem=send, recv_sem=recv, device_id=target, device_id_type=MESH
        )

    def z_copy(j, target):
        part = full.at[SLOTS + j, :, :, cols(target[1], c)]
        return remote(staged.at[j], part, z_send.at[j], z_recv.at[j], target)

    def start_direct(j):
        z_copy(j, behind(b, offset_of(j))).start()

    def relay_copy(k):
        j = UNIT_OF[HALF_WAY, k]
        return remote(staged.at[j], passing.at[k], z_send.at[j], n_recv.at[k], relay_to)

    def pass_copy(k):
        j = UNIT_OF[HALF_WAY, k]
        part = full.at[SLOTS + j, :, :, cols(passed_to[1], c)]
        return remote(passing.at[k], part, n_send.at[k], z_recv.at[j], passed_to)

    for count, j in enumerate(RELAYED[:1] + DIRECT[:1] + RELAYED[1:] + DIRECT[1:]):
        k, o = j // HOPS, offset_of(j)
        block = jnp.clip(starts[o] + jnp.minimum(k, blocks[o] - 1), 0, x_quarter.shape[1] - 1)
        y_of = behind(b, o)[1]
        staged[j, 0] = x_quarter[y_of, block]
        live = row_id < live_of[o] - k * BLOCK
        staged[j, 1] = jnp.where(live, g_quarter[y_of, block], jnp.zeros((), jnp.bfloat16))
        if count == 0:
            pl.semaphore_wait(barrier, len(senders))
        if o == HALF_WAY:
            relay_copy(k).start()
        elif j in DIRECT[:IN_FLIGHT]:
            start_direct(j)

    for load in loads[4:-1]:
        load.wait()
    for k in range(SLOTS):
        live = row_id < live_of[0] - k * BLOCK
        full[k, 1] = jnp.where(live, full[k, 1], jnp.zeros((), jnp.bfloat16))
    grad_in[...] = jnp.zeros_like(grad_in)
    grad_out[...] = jnp.zeros_like(grad_out)

    def y_copy(j):
        part = full.at[SLOTS + j, :, :, own]
        return remote(part, part, y_send.at[j], y_recv.at[j], y_peer)

    def c_copy(j):
        part = full.at[SLOTS + j, :, :, own]
        return remote(part, part, c_send.at[j], c_recv.at[j], c_peer)

    def d_copy(j):
        part = full.at[SLOTS + j, :, :, cols(1 - y, c)]
        return remote(part, part, d_send.at[j], d_recv.at[j], c_peer)

    def p_copy(u):
        return remote(pieces.at[u, 1 - c], pieces_in.at[u], p_send.at[u], p_recv.at[u], c_peer)

    def h_copy(u):
        return remote(half_out.at[u], half_in.at[u], h_send.at[u], h_recv.at[u], y_peer)

    def r_copy(j):
        return remote(home_out.at[j], home.at[SLOTS + j], r_send.at[j], r_recv.at[j], ahead(b, offset_of(j)))

    def finished_by(u):
        away = (u + UNITS - SLOTS) // UNITS
        return ahead(b, away * offset_of(u - away * SLOTS))[1]

    def compute(u):
        rows_in, rows_cot = full[u, 0], full[u, 1]
        projected = contract_last(rows_in, w_in[...])
        gate_pre, up_pre = projected[:, :unit_count], projected[:, unit_count:]
        sigmoid_gate = jax.nn.sigmoid(gate_pre)
        active = gate_pre * sigmoid_gate
        hidden = (active * up_pre).astype(jnp.bfloat16)
        hidden_grad = contract_last(rows_cot, w_out[...])
        gate_grad = hidden_grad * up_pre * sigmoid_gate * (1.0 + gate_pre * (1.0 - sigmoid_gate))
        both = jnp.concatenate([gate_grad, hidden_grad * active], axis=1).astype(jnp.bfloat16)
        for q in range(4):
            pieces[u, q % 2, q // 2] = jnp.dot(
                both, w_in[:, q * quarter : (q + 1) * quarter], preferred_element_type=jnp.float32
            ).astype(jnp.bfloat16)
        p_copy(u).start()
        grad_in[...] += contract_first(both, rows_in)
        grad_out[...] += contract_first(hidden, rows_cot)

    def partial_sum(u, y_of):
        return pieces[u, c, y_of].astype(jnp.float32) + pieces_in[u, y_of].astype(jnp.float32)

    def step(s, carry):
        for i, j in enumerate(DIRECT[IN_FLIGHT:]):

            @pl.when(s == i + 2)
            def _():
                z_copy(DIRECT[i], y_peer).wait_send()
                start_direct(j)

        @pl.when(s >= 2)
        def _():
            u = s - 2
            h_copy(u).wait_recv()
            total = (partial_sum(u, finished_by(u)) + half_in[u].astype(jnp.float32)).astype(jnp.bfloat16)

            @pl.when(u < SLOTS)
            def _():
                home[u] = total

            @pl.when(u >= SLOTS)
            def _():
                home_out[u - SLOTS] = total
                r_copy(u - SLOTS).start()

        @pl.when((s >= 1) & (s < UNITS + 1))
        def _():
            u = s - 1
            p_copy(u).wait_recv()
            half_out[u] = partial_sum(u, 1 - finished_by(u)).astype(jnp.bfloat16)
            h_copy(u).start()

        @pl.when(s < UNITS)
        def _():
            @pl.when(s >= SLOTS)
            def _():
                c_copy(s - SLOTS).wait_recv()
                d_copy(s - SLOTS).wait_recv()

            compute(s)

        @pl.when((s + 1 >= SLOTS) & (s + 1 < UNITS))
        def _():
            j = s + 1 - SLOTS
            y_copy(j).wait_recv()
            d_copy(j).start()

        for k in range(SLOTS):

            @pl.when(s == k)
            def _():
                relay_copy(k).wait_recv()
                pass_copy(k).start()

        @pl.when((s + 2 >= SLOTS) & (s + 2 < UNITS))
        def _():
            j = s + 2 - SLOTS
            z_copy(j, y_peer).wait_recv()
            y_copy(j).start()
            c_copy(j).start()

        return carry

    lax.fori_loop(0, UNITS + 2, step, 0)

    for j in RELAYED + DIRECT[-IN_FLIGHT:]:
        z_copy(j, y_peer).wait_send()
    for k in range(SLOTS):
        pass_copy(k).wait_send()

    def drain(j, carry):
        r_copy(j).wait_recv()
        y_copy(j).wait_send()
        c_copy(j).wait_send()
        d_copy(j).wait_send()
        r_copy(j).wait_send()
        return carry

    lax.fori_loop(0, REMOTE, drain, 0)

    def drain_sums(u, carry):
        p_copy(u).wait_send()
        h_copy(u).wait_send()
        return carry

    lax.fori_loop(0, UNITS, drain_sums, 0)

    for p in range(grad_x.shape[0] // BLOCK):
        unit = jnp.int32(0)
        for o in range(HOPS + 1):
            for k in range(SLOTS):
                here = k if o == 0 else SLOTS + UNIT_OF[o, k]
                unit = jnp.where((starts[o] + k == p) & (k < blocks[o]), here, unit)
        grad_x[pl.ds(p * BLOCK, BLOCK), :] = home[jnp.clip(unit, 0, UNITS - 1)]


def on_device(x_rows, grad_rows, w_gate_up, w_down, counts):
    rows, features = x_rows.shape
    units = w_down.shape[1]
    quarter = features // 4
    vmem = pl.BlockSpec(memory_space=pltpu.VMEM)
    held = pl.BlockSpec(memory_space=pl.ANY)
    b16, f32 = jnp.bfloat16, jnp.float32
    dma = pltpu.SemaphoreType.DMA
    grad_in, grad_out, grad_x = pl.pallas_call(
        lambda *refs: kernel(lax.axis_size("blk"), *refs),
        name="experts_backward",
        out_shape=(
            jax.ShapeDtypeStruct((2 * units, features), f32),
            jax.ShapeDtypeStruct((units, features), f32),
            jax.ShapeDtypeStruct((rows, quarter), b16),
        ),
        in_specs=[held, held, held, vmem, vmem],
        out_specs=(vmem, vmem, vmem),
        scratch_shapes=[
            pltpu.VMEM((2, rows // BLOCK, BLOCK, quarter), b16),
            pltpu.VMEM((2, rows // BLOCK, BLOCK, quarter), b16),
            pltpu.VMEM((REMOTE, 2, BLOCK, quarter), b16),
            pltpu.VMEM((SLOTS, 2, BLOCK, quarter), b16),
            pltpu.VMEM((UNITS, 2, BLOCK, features), b16),
            pltpu.VMEM((UNITS, 2, 2, BLOCK, quarter), b16),
            pltpu.VMEM((UNITS, 2, BLOCK, quarter), b16),
            pltpu.VMEM((UNITS, BLOCK, quarter), b16),
            pltpu.VMEM((UNITS, BLOCK, quarter), b16),
            pltpu.VMEM((REMOTE, BLOCK, quarter), b16),
            pltpu.VMEM((UNITS, BLOCK, quarter), b16),
            pltpu.SMEM(counts.shape[::-1], counts.dtype),
            dma((5 + 2 * SLOTS,)),
            *[dma((REMOTE,))] * 2,
            *[dma((SLOTS,))] * 2,
            *[dma((REMOTE,))] * 6,
            *[dma((UNITS,))] * 4,
            *[dma((REMOTE,))] * 2,
        ],
        compiler_params=pltpu.CompilerParams(
            collective_id=0, has_side_effects=True, vmem_limit_bytes=60 * 1024 * 1024
        ),
    )(
        counts.T,
        x_rows.reshape(-1, BLOCK, features),
        grad_rows.reshape(-1, BLOCK, features),
        w_gate_up.reshape(2 * units, features),
        w_down.reshape(units, features),
    )
    return (grad_in.reshape(1, 2, units, features), grad_out[None], grad_x)


def solution(mesh):
    finer = Mesh(mesh.devices.reshape(mesh.shape["blk"], 2, 2), ("blk", "dp_0", "dp_1"))
    placed = (P("blk", None), P("blk", None), P("blk", None, DP, None), P("blk", DP, None), P())
    return jax.shard_map(
        on_device,
        mesh=finer,
        in_specs=placed,
        out_specs=(P("blk", None, DP, None), P("blk", DP, None), P("blk", DP)),
        check_vma=False,
    )
```

```python
import jax
import jax.numpy as jnp
from jax import lax
from jax.experimental import pallas as pl
from jax.experimental.pallas import tpu as pltpu
from jax.sharding import Mesh
from jax.sharding import PartitionSpec as P

HOPS = 4
BLOCK = 128
SLOTS = 3
DP = ("dp_0", "dp_1")
MESH = pl.DeviceIdType.MESH
UNITS = SLOTS * (HOPS + 1)
REMOTE = SLOTS * HOPS


def contract_last(lhs, rhs):
    return lax.dot_general(lhs, rhs, (((1,), (1,)), ((), ())), preferred_element_type=jnp.float32)


def contract_first(lhs, rhs):
    return lax.dot_general(lhs, rhs, (((0,), (0,)), ((), ())), preferred_element_type=jnp.float32)


HALF_WAY = HOPS
COLUMN = 8
HALF = 32
FIRSTS = HOPS
EXTRAS = 3


def offset_of(j):
    late = (j // FIRSTS + 1) // 2
    pair = (j - late * FIRSTS) // 2
    return (1 - late) * (j + 1 + j // 2 - 2 * (j // 3)) + late * (1 + (HOPS - pair) % HOPS)


def rank_of(j):
    return 0 if j < FIRSTS else 1 + j % 2


UNIT_OF = {(offset_of(j), rank_of(j)): j for j in range(REMOTE)}
FAR = UNIT_OF[HALF_WAY, 0]


def kernel(
    n_blk,
    counts_hbm,
    x_hbm,
    g_hbm,
    w_in,
    w_out,
    grad_in,
    grad_out,
    grad_x,
    x_quarter,
    g_quarter,
    staged,
    passing,
    past_1,
    past_2,
    past_3,
    past_4,
    full,
    pieces,
    pieces_in,
    half_out,
    half_in,
    home_out,
    home,
    counts,
    load_sem,
    z_send,
    z_recv,
    n_send,
    n_recv,
    m_send,
    m_recv,
    e_send,
    e_recv,
    y_send,
    y_recv,
    c_send,
    c_recv,
    d_send,
    d_recv,
    p_send,
    p_recv,
    h_send,
    h_recv,
    r_send,
    r_recv,
):
    b, y, c = lax.axis_index("blk"), lax.axis_index("dp_0"), lax.axis_index("dp_1")
    unit_count = w_out.shape[0]
    quarter = x_quarter.shape[2]

    def up(position, steps):
        level = lax.rem(position, COLUMN)
        return position - level + lax.rem(level + steps, COLUMN)

    def behind(position, o):
        crossed = 1 - (lax.rem(position, HALF) - o + HALF) // HALF
        return (lax.rem(position - o + n_blk, n_blk), y + crossed * (1 - 2 * y), c)

    def ahead(position, o):
        crossed = (lax.rem(position, HALF) + o) // HALF
        return (lax.rem(position + o, n_blk), y + crossed * (1 - 2 * y), c)

    y_peer, c_peer = (b, 1 - y, c), (b, y, 1 - c)
    relay_to = (up(b, 1), y, c)
    passed_to = behind(up(b, COLUMN - 1), HALF_WAY)

    def cols(y_of, c_of):
        return pl.ds(pl.multiple_of((2 * y_of + c_of) * quarter, quarter), quarter)

    own = cols(y, c)
    loads = []
    for held, source in ((x_quarter, x_hbm), (g_quarter, g_hbm)):
        loads.append(pltpu.make_async_copy(source.at[:, :, own], held, load_sem.at[len(loads)]))
    for k in range(SLOTS):
        for held, source in ((0, x_hbm), (1, g_hbm)):
            loads.append(pltpu.make_async_copy(source.at[k], full.at[k, held], load_sem.at[len(loads)]))
    loads.append(pltpu.make_async_copy(counts_hbm, counts, load_sem.at[len(loads)]))
    for load in loads:
        load.start()

    barrier = pltpu.get_barrier_semaphore()
    senders = [ahead(b, o) for o in range(1, HALF_WAY)] + [behind(b, o) for o in range(1, HOPS + 1)]
    home_of_far = ahead(b, HALF_WAY)
    senders += [(up(b, COLUMN - 1), y, c), (up(home_of_far[0], 1), home_of_far[1], c), y_peer, c_peer]
    for sender in senders:
        pl.semaphore_signal(barrier, 1, device_id=sender, device_id_type=MESH)

    for load in (*loads[:2], loads[-1]):
        load.wait()
    def split(position):
        live = [counts[o, position] for o in range(HOPS + 1)]
        blocks = [lax.shift_right_logical(n + (BLOCK - 1), 7) for n in live]
        starts, before = [jnp.int32(0)], [jnp.int32(0)]
        for o in range(HOPS):
            starts.append(starts[o] + blocks[o])
            before.append(before[o] + blocks[o] - 1)
        return live, blocks, starts, before

    live_of, blocks, starts, before = split(b)
    row_id = lax.broadcasted_iota(jnp.int32, (BLOCK, 1), 0)

    def remote(src, dst, send, recv, target):
        return pltpu.make_async_remote_copy(
            src_ref=src, dst_ref=dst, send_sem=send, recv_sem=recv, device_id=target, device_id_type=MESH
        )

    past = (past_1, past_2, past_3, past_4)

    def z_copy(j, target):
        return remote(staged.at[j], full.at[SLOTS + j, :, :, own], z_send.at[j], z_recv.at[j], target)

    def extra_copy(hop, t):
        source = staged.at[FIRSTS + t] if hop == 0 else past[hop - 1].at[t]
        at = hop * EXTRAS + t
        return remote(source, past[hop].at[t], e_send.at[at], e_recv.at[at], behind(b, 1))

    def relay_copy(k):
        source = staged.at[FAR if k == 0 else FIRSTS + k]
        return remote(source, passing.at[k], n_send.at[k], n_recv.at[k], relay_to)

    def pass_copy(k):
        part = full.at[SLOTS + FAR, :, :, own] if k == 0 else past_4.at[k - 1]
        landed = z_recv.at[FAR] if k == 0 else m_recv.at[k]
        return remote(passing.at[k], part, m_send.at[k], landed, passed_to)

    def place(slot, block):
        block = jnp.clip(block, 0, x_quarter.shape[0] - 1)
        staged[slot, 0] = x_quarter[block]
        return g_quarter[block]

    zero = jnp.zeros((), jnp.bfloat16)
    for j in range(FIRSTS):
        o = offset_of(j)
        staged[j, 1] = jnp.where(row_id < live_of[o], place(j, starts[o]), zero)
        if j == 0:
            pl.semaphore_wait(barrier, len(senders))
        if o == HALF_WAY:
            relay_copy(0).start()
        else:
            z_copy(j, behind(b, o)).start()
    for t in range(EXTRAS):
        block = jnp.int32(0)
        for o in range(HOPS + 1):
            at = t - before[o]
            block = jnp.where((at >= 0) & (at < blocks[o] - 1), starts[o] + 1 + at, block)
        staged[FIRSTS + t, 1] = place(FIRSTS + t, block)
        extra_copy(0, t).start()
        if t > 0:
            relay_copy(t).start()

    for load in loads[2:-1]:
        load.wait()
    for k in range(SLOTS):
        live = row_id < live_of[0] - k * BLOCK
        full[k, 1] = jnp.where(live, full[k, 1], jnp.zeros((), jnp.bfloat16))
    grad_in[...] = jnp.zeros_like(grad_in)
    grad_out[...] = jnp.zeros_like(grad_out)

    def y_copy(j):
        part = full.at[SLOTS + j, :, :, cols(ahead(b, offset_of(j))[1], c)]
        return remote(part, part, y_send.at[j], y_recv.at[j], y_peer)

    def c_copy(j):
        part = full.at[SLOTS + j, :, :, cols(ahead(b, offset_of(j))[1], c)]
        return remote(part, part, c_send.at[j], c_recv.at[j], c_peer)

    def d_copy(j):
        part = full.at[SLOTS + j, :, :, cols(1 - ahead(b, offset_of(j))[1], c)]
        return remote(part, part, d_send.at[j], d_recv.at[j], c_peer)

    def spread(j):
        y_copy(j).start()
        c_copy(j).start()

    def pick(j):
        o, k = offset_of(j), rank_of(j)
        home_of, y_of, _ = ahead(b, o)
        live, _, _, first = split(home_of)
        lowest = 1 if o == HALF_WAY else 0
        t = jnp.clip(first[o] + k - 1, lowest, EXTRAS - 1) - lowest
        part = cols(y_of, c)
        full[SLOTS + j, 0, :, part] = past[o - 1][t, 0]
        full[SLOTS + j, 1, :, part] = jnp.where(row_id < live[o] - k * BLOCK, past[o - 1][t, 1], zero)
        spread(j)

    def p_copy(u):
        return remote(pieces.at[u, 1 - c], pieces_in.at[u], p_send.at[u], p_recv.at[u], c_peer)

    def h_copy(u):
        return remote(half_out.at[u], half_in.at[u], h_send.at[u], h_recv.at[u], y_peer)

    def r_copy(j):
        return remote(home_out.at[j], home.at[SLOTS + j], r_send.at[j], r_recv.at[j], ahead(b, offset_of(j)))

    def finished_by(u):
        away = (u + UNITS - SLOTS) // UNITS
        return ahead(b, away * offset_of(u - away * SLOTS))[1]

    def compute(u):
        rows_in, rows_cot = full[u, 0], full[u, 1]
        projected = contract_last(rows_in, w_in[...])
        gate_pre, up_pre = projected[:, :unit_count], projected[:, unit_count:]
        sigmoid_gate = jax.nn.sigmoid(gate_pre)
        active = gate_pre * sigmoid_gate
        hidden = (active * up_pre).astype(jnp.bfloat16)
        hidden_grad = contract_last(rows_cot, w_out[...])
        gate_grad = hidden_grad * up_pre * sigmoid_gate * (1.0 + gate_pre * (1.0 - sigmoid_gate))
        both = jnp.concatenate([gate_grad, hidden_grad * active], axis=1).astype(jnp.bfloat16)
        for q in range(4):
            pieces[u, q % 2, q // 2] = jnp.dot(
                both, w_in[:, q * quarter : (q + 1) * quarter], preferred_element_type=jnp.float32
            ).astype(jnp.bfloat16)
        p_copy(u).start()
        grad_in[...] += contract_first(both, rows_in)
        grad_out[...] += contract_first(hidden, rows_cot)

    def partial_sum(u, y_of):
        return pieces[u, c, y_of].astype(jnp.float32) + pieces_in[u, y_of].astype(jnp.float32)

    def step(s, carry):
        def forward(at, hop, t):
            @pl.when(s == at)
            def _():
                extra_copy(hop - 1, t).wait_recv()
                extra_copy(hop, t).start()

        @pl.when(s >= 2)
        def _():
            u = s - 2
            h_copy(u).wait_recv()
            total = (partial_sum(u, finished_by(u)) + half_in[u].astype(jnp.float32)).astype(jnp.bfloat16)

            @pl.when(u < SLOTS)
            def _():
                home[u] = total

            @pl.when(u >= SLOTS)
            def _():
                home_out[u - SLOTS] = total
                r_copy(u - SLOTS).start()

        @pl.when((s >= 1) & (s < UNITS + 1))
        def _():
            u = s - 1
            p_copy(u).wait_recv()
            half_out[u] = partial_sum(u, 1 - finished_by(u)).astype(jnp.bfloat16)
            h_copy(u).start()

        forward(7, 2, 0)
        forward(8, 2, 1)

        @pl.when(s < UNITS)
        def _():
            @pl.when(s >= SLOTS)
            def _():
                c_copy(s - SLOTS).wait_recv()
                d_copy(s - SLOTS).wait_recv()

            compute(s)

        forward(8, 2, 2)

        @pl.when((s + 1 >= SLOTS) & (s + 1 < UNITS))
        def _():
            j = s + 1 - SLOTS
            y_copy(j).wait_recv()
            d_copy(j).start()

        for k in range(SLOTS):

            @pl.when(s == k)
            def _():
                relay_copy(k).wait_recv()
                pass_copy(k).start()

        @pl.when((s + 2 >= SLOTS) & (s + 2 < SLOTS + FIRSTS))
        def _():
            j = s + 2 - SLOTS
            z_copy(j, y_peer).wait_recv()
            spread(j)

        forward(4, 1, 0)
        forward(5, 1, 1)
        forward(5, 1, 2)
        for j in range(FIRSTS, REMOTE):

            @pl.when(s + 2 == SLOTS + j)
            def _():
                if rank_of(j) == 1 and offset_of(j) == 3:
                    for t in range(EXTRAS):
                        extra_copy(2, t).wait_recv()
                if rank_of(j) == 1 and offset_of(j) == HALF_WAY:
                    for k in range(1, SLOTS):
                        pass_copy(k).wait_recv()
                pick(j)

        return carry

    lax.fori_loop(0, UNITS + 2, step, 0)

    for j in range(FIRSTS):
        if j != FAR:
            z_copy(j, y_peer).wait_send()
    for hop in range(3):
        for t in range(EXTRAS):
            extra_copy(hop, t).wait_send()
    for k in range(SLOTS):
        relay_copy(k).wait_send()
        pass_copy(k).wait_send()

    def drain(j, carry):
        r_copy(j).wait_recv()
        y_copy(j).wait_send()
        c_copy(j).wait_send()
        d_copy(j).wait_send()
        r_copy(j).wait_send()
        return carry

    lax.fori_loop(0, REMOTE, drain, 0)

    def drain_sums(u, carry):
        p_copy(u).wait_send()
        h_copy(u).wait_send()
        return carry

    lax.fori_loop(0, UNITS, drain_sums, 0)

    for p in range(grad_x.shape[0] // BLOCK):
        unit = jnp.int32(0)
        for o in range(HOPS + 1):
            for k in range(SLOTS):
                here = k if o == 0 else SLOTS + UNIT_OF[o, k]
                unit = jnp.where((starts[o] + k == p) & (k < blocks[o]), here, unit)
        grad_x[pl.ds(p * BLOCK, BLOCK), :] = home[jnp.clip(unit, 0, UNITS - 1)]


def on_device(x_rows, grad_rows, w_gate_up, w_down, counts):
    rows, features = x_rows.shape
    units = w_down.shape[1]
    quarter = features // 4
    vmem = pl.BlockSpec(memory_space=pltpu.VMEM)
    held = pl.BlockSpec(memory_space=pl.ANY)
    b16, f32 = jnp.bfloat16, jnp.float32
    dma = pltpu.SemaphoreType.DMA
    grad_in, grad_out, grad_x = pl.pallas_call(
        lambda *refs: kernel(lax.axis_size("blk"), *refs),
        name="experts_backward",
        out_shape=(
            jax.ShapeDtypeStruct((2 * units, features), f32),
            jax.ShapeDtypeStruct((units, features), f32),
            jax.ShapeDtypeStruct((rows, quarter), b16),
        ),
        in_specs=[held, held, held, vmem, vmem],
        out_specs=(vmem, vmem, vmem),
        scratch_shapes=[
            pltpu.VMEM((rows // BLOCK, BLOCK, quarter), b16),
            pltpu.VMEM((rows // BLOCK, BLOCK, quarter), b16),
            pltpu.VMEM((FIRSTS + EXTRAS, 2, BLOCK, quarter), b16),
            pltpu.VMEM((SLOTS, 2, BLOCK, quarter), b16),
            *[pltpu.VMEM((EXTRAS, 2, BLOCK, quarter), b16)] * 3,
            pltpu.VMEM((EXTRAS - 1, 2, BLOCK, quarter), b16),
            pltpu.VMEM((UNITS, 2, BLOCK, features), b16),
            pltpu.VMEM((UNITS, 2, 2, BLOCK, quarter), b16),
            pltpu.VMEM((UNITS, 2, BLOCK, quarter), b16),
            pltpu.VMEM((UNITS, BLOCK, quarter), b16),
            pltpu.VMEM((UNITS, BLOCK, quarter), b16),
            pltpu.VMEM((REMOTE, BLOCK, quarter), b16),
            pltpu.VMEM((UNITS, BLOCK, quarter), b16),
            pltpu.SMEM(counts.shape[::-1], counts.dtype),
            dma((3 + 2 * SLOTS,)),
            *[dma((FIRSTS,))] * 2,
            *[dma((SLOTS,))] * 4,
            *[dma((3 * EXTRAS,))] * 2,
            *[dma((REMOTE,))] * 6,
            *[dma((UNITS,))] * 4,
            *[dma((REMOTE,))] * 2,
        ],
        compiler_params=pltpu.CompilerParams(
            collective_id=0, has_side_effects=True, vmem_limit_bytes=60 * 1024 * 1024
        ),
    )(
        counts.T,
        x_rows.reshape(-1, BLOCK, features),
        grad_rows.reshape(-1, BLOCK, features),
        w_gate_up.reshape(2 * units, features),
        w_down.reshape(units, features),
    )
    return (grad_in.reshape(1, 2, units, features), grad_out[None], grad_x)


def solution(mesh):
    finer = Mesh(mesh.devices.reshape(mesh.shape["blk"], 2, 2), ("blk", "dp_0", "dp_1"))
    placed = (P("blk", None), P("blk", None), P("blk", None, DP, None), P("blk", DP, None), P())
    return jax.shard_map(
        on_device,
        mesh=finer,
        in_specs=placed,
        out_specs=(P("blk", None, DP, None), P("blk", DP, None), P("blk", DP)),
        check_vma=False,
    )
```

```python
import jax
import jax.numpy as jnp
from jax import lax
from jax.experimental import pallas as pl
from jax.experimental.pallas import tpu as pltpu
from jax.sharding import Mesh
from jax.sharding import PartitionSpec as P

HOPS = 4
BLOCK = 128
SLOTS = 3
DP = ("dp_0", "dp_1")
MESH = pl.DeviceIdType.MESH
UNITS = SLOTS * (HOPS + 1)
REMOTE = SLOTS * HOPS


def contract_last(lhs, rhs):
    return lax.dot_general(lhs, rhs, (((1,), (1,)), ((), ())), preferred_element_type=jnp.float32)


def contract_first(lhs, rhs):
    return lax.dot_general(lhs, rhs, (((0,), (0,)), ((), ())), preferred_element_type=jnp.float32)


HALF_WAY = HOPS
COLUMN = 8
HALF = 32
FIRSTS = HOPS
EXTRAS = 3


def offset_of(j):
    def since(first):
        return (j + REMOTE - first) // REMOTE

    return 1 + 3 * since(1) - 3 * since(2) + since(4) + 2 * since(7) - since(9)


RANKS = (0, 0, 1, 2, 0, 1, 2, 1, 2, 0, 1, 2)
UNIT_OF = {(offset_of(j), RANKS[j]): j for j in range(REMOTE)}
FAR = UNIT_OF[HALF_WAY, 0]


def kernel(
    n_blk,
    counts_hbm,
    x_hbm,
    g_hbm,
    w_in,
    w_out,
    grad_in,
    grad_out,
    grad_x,
    x_quarter,
    g_quarter,
    staged,
    passing,
    past_1,
    past_2,
    past_3,
    past_4,
    full,
    pieces,
    pieces_in,
    half_out,
    half_in,
    home_out,
    home,
    counts,
    load_sem,
    z_send,
    z_recv,
    n_send,
    n_recv,
    m_send,
    m_recv,
    e_send,
    e_recv,
    y_send,
    y_recv,
    c_send,
    c_recv,
    d_send,
    d_recv,
    p_send,
    p_recv,
    h_send,
    h_recv,
    r_send,
    r_recv,
):
    b, y, c = lax.axis_index("blk"), lax.axis_index("dp_0"), lax.axis_index("dp_1")
    unit_count = w_out.shape[0]
    quarter = x_quarter.shape[2]

    def up(position, steps):
        level = lax.rem(position, COLUMN)
        return position - level + lax.rem(level + steps, COLUMN)

    def behind(position, o):
        crossed = 1 - (lax.rem(position, HALF) - o + HALF) // HALF
        return (lax.rem(position - o + n_blk, n_blk), y + crossed * (1 - 2 * y), c)

    def ahead(position, o):
        crossed = (lax.rem(position, HALF) + o) // HALF
        return (lax.rem(position + o, n_blk), y + crossed * (1 - 2 * y), c)

    y_peer, c_peer = (b, 1 - y, c), (b, y, 1 - c)
    relay_to = (up(b, 1), y, c)
    passed_to = behind(up(b, COLUMN - 1), HALF_WAY)

    def cols(y_of, c_of):
        return pl.ds(pl.multiple_of((2 * y_of + c_of) * quarter, quarter), quarter)

    own = cols(y, c)
    loads = []
    for held, source in ((x_quarter, x_hbm), (g_quarter, g_hbm)):
        loads.append(pltpu.make_async_copy(source.at[:, :, own], held, load_sem.at[len(loads)]))
    for k in range(SLOTS):
        for held, source in ((0, x_hbm), (1, g_hbm)):
            loads.append(pltpu.make_async_copy(source.at[k], full.at[k, held], load_sem.at[len(loads)]))
    loads.append(pltpu.make_async_copy(counts_hbm, counts, load_sem.at[len(loads)]))
    for load in loads:
        load.start()

    barrier = pltpu.get_barrier_semaphore()
    senders = [ahead(b, o) for o in range(1, HALF_WAY)] + [behind(b, o) for o in range(1, HOPS + 1)]
    home_of_far = ahead(b, HALF_WAY)
    senders += [(up(b, COLUMN - 1), y, c), (up(home_of_far[0], 1), home_of_far[1], c), y_peer, c_peer]
    for sender in senders:
        pl.semaphore_signal(barrier, 1, device_id=sender, device_id_type=MESH)

    for load in (*loads[:2], loads[-1]):
        load.wait()
    def split(position):
        live = [counts[o, position] for o in range(HOPS + 1)]
        blocks = [lax.shift_right_logical(n + (BLOCK - 1), 7) for n in live]
        starts, before = [jnp.int32(0)], [jnp.int32(0)]
        for o in range(HOPS):
            starts.append(starts[o] + blocks[o])
            before.append(before[o] + blocks[o] - 1)
        return live, blocks, starts, before

    live_of, blocks, starts, before = split(b)
    row_id = lax.broadcasted_iota(jnp.int32, (BLOCK, 1), 0)

    def remote(src, dst, send, recv, target):
        return pltpu.make_async_remote_copy(
            src_ref=src, dst_ref=dst, send_sem=send, recv_sem=recv, device_id=target, device_id_type=MESH
        )

    past = (past_1, past_2, past_3, past_4)

    def z_copy(o):
        part = full.at[SLOTS + UNIT_OF[o, 0], :, :, own]
        return remote(staged.at[o - 1], part, z_send.at[o - 1], z_recv.at[o - 1], behind(b, o))

    def extra_copy(hop, t):
        source = staged.at[FIRSTS + t] if hop == 0 else past[hop - 1].at[t]
        at = hop * EXTRAS + t
        return remote(source, past[hop].at[t], e_send.at[at], e_recv.at[at], behind(b, 1))

    def relay_copy(k):
        source = staged.at[HALF_WAY - 1 if k == 0 else FIRSTS + k]
        return remote(source, passing.at[k], n_send.at[k], n_recv.at[k], relay_to)

    def pass_copy(k):
        part = full.at[SLOTS + FAR, :, :, own] if k == 0 else past_4.at[k - 1]
        landed = z_recv.at[HALF_WAY - 1] if k == 0 else m_recv.at[k]
        return remote(passing.at[k], part, m_send.at[k], landed, passed_to)

    def place(slot, block):
        block = jnp.clip(block, 0, x_quarter.shape[0] - 1)
        staged[slot, 0] = x_quarter[block]
        return g_quarter[block]

    zero = jnp.zeros((), jnp.bfloat16)
    def place_first(o):
        staged[o - 1, 1] = jnp.where(row_id < live_of[o], place(o - 1, starts[o]), zero)

    place_first(1)
    pl.semaphore_wait(barrier, len(senders))
    z_copy(1).start()
    place_first(HALF_WAY)
    relay_copy(0).start()
    for t in range(EXTRAS):
        block = jnp.int32(0)
        for o in range(HOPS + 1):
            at = t - before[o]
            block = jnp.where((at >= 0) & (at < blocks[o] - 1), starts[o] + 1 + at, block)
        staged[FIRSTS + t, 1] = place(FIRSTS + t, block)
        extra_copy(0, t).start()
    place_first(2)
    place_first(3)

    for load in loads[2:-1]:
        load.wait()
    for k in range(SLOTS):
        live = row_id < live_of[0] - k * BLOCK
        full[k, 1] = jnp.where(live, full[k, 1], jnp.zeros((), jnp.bfloat16))
    grad_in[...] = jnp.zeros_like(grad_in)
    grad_out[...] = jnp.zeros_like(grad_out)

    def y_copy(j):
        part = full.at[SLOTS + j, :, :, cols(ahead(b, offset_of(j))[1], c)]
        return remote(part, part, y_send.at[j], y_recv.at[j], y_peer)

    def c_copy(j):
        part = full.at[SLOTS + j, :, :, cols(ahead(b, offset_of(j))[1], c)]
        return remote(part, part, c_send.at[j], c_recv.at[j], c_peer)

    def d_copy(j):
        part = full.at[SLOTS + j, :, :, cols(1 - ahead(b, offset_of(j))[1], c)]
        return remote(part, part, d_send.at[j], d_recv.at[j], c_peer)

    def spread(j):
        y_copy(j).start()
        c_copy(j).start()

    def pick(j):
        o, k = offset_of(j), RANKS[j]
        home_of, y_of, _ = ahead(b, o)
        live, _, _, first = split(home_of)
        lowest = 1 if o == HALF_WAY else 0
        t = jnp.clip(first[o] + k - 1, lowest, EXTRAS - 1) - lowest
        part = cols(y_of, c)
        full[SLOTS + j, 0, :, part] = past[o - 1][t, 0]
        full[SLOTS + j, 1, :, part] = jnp.where(row_id < live[o] - k * BLOCK, past[o - 1][t, 1], zero)
        spread(j)

    def p_copy(u):
        return remote(pieces.at[u, 1 - c], pieces_in.at[u], p_send.at[u], p_recv.at[u], c_peer)

    def h_copy(u):
        return remote(half_out.at[u], half_in.at[u], h_send.at[u], h_recv.at[u], y_peer)

    def r_copy(j):
        return remote(home_out.at[j], home.at[SLOTS + j], r_send.at[j], r_recv.at[j], ahead(b, offset_of(j)))

    def finished_by(u):
        away = (u + UNITS - SLOTS) // UNITS
        return ahead(b, away * offset_of(u - away * SLOTS))[1]

    def compute(u):
        rows_in, rows_cot = full[u, 0], full[u, 1]
        projected = contract_last(rows_in, w_in[...])
        gate_pre, up_pre = projected[:, :unit_count], projected[:, unit_count:]
        sigmoid_gate = jax.nn.sigmoid(gate_pre)
        active = gate_pre * sigmoid_gate
        hidden = (active * up_pre).astype(jnp.bfloat16)
        hidden_grad = contract_last(rows_cot, w_out[...])
        gate_grad = hidden_grad * up_pre * sigmoid_gate * (1.0 + gate_pre * (1.0 - sigmoid_gate))
        both = jnp.concatenate([gate_grad, hidden_grad * active], axis=1).astype(jnp.bfloat16)
        for q in range(4):
            pieces[u, q % 2, q // 2] = jnp.dot(
                both, w_in[:, q * quarter : (q + 1) * quarter], preferred_element_type=jnp.float32
            ).astype(jnp.bfloat16)
        p_copy(u).start()
        grad_in[...] += contract_first(both, rows_in)
        grad_out[...] += contract_first(hidden, rows_cot)

    def partial_sum(u, y_of):
        return pieces[u, c, y_of].astype(jnp.float32) + pieces_in[u, y_of].astype(jnp.float32)

    def step(s, carry):
        def forward(at, hop, t):
            @pl.when(s == at)
            def _():
                extra_copy(hop - 1, t).wait_recv()
                extra_copy(hop, t).start()

        def relay(at, k):
            @pl.when(s == at)
            def _():
                relay_copy(k).wait_recv()
                pass_copy(k).start()
                if k == 0:
                    relay_copy(1).start()
                    relay_copy(2).start()

        def start_first(at, o):
            @pl.when(s == at)
            def _():
                z_copy(o).start()

        @pl.when(s >= 2)
        def _():
            u = s - 2
            h_copy(u).wait_recv()
            total = (partial_sum(u, finished_by(u)) + half_in[u].astype(jnp.float32)).astype(jnp.bfloat16)

            @pl.when(u < SLOTS)
            def _():
                home[u] = total

            @pl.when(u >= SLOTS)
            def _():
                home_out[u - SLOTS] = total
                r_copy(u - SLOTS).start()

        @pl.when((s >= 1) & (s < UNITS + 1))
        def _():
            u = s - 1
            p_copy(u).wait_recv()
            half_out[u] = partial_sum(u, 1 - finished_by(u)).astype(jnp.bfloat16)
            h_copy(u).start()

        @pl.when(s < UNITS)
        def _():
            @pl.when(s >= SLOTS)
            def _():
                c_copy(s - SLOTS).wait_recv()
                d_copy(s - SLOTS).wait_recv()

            compute(s)

        forward(3, 1, 2)
        relay(3, 2)
        forward(5, 2, 0)
        forward(6, 2, 1)

        @pl.when((s + 1 >= SLOTS) & (s + 1 < UNITS))
        def _():
            j = s + 1 - SLOTS
            y_copy(j).wait_recv()
            d_copy(j).start()

        relay(0, 0)
        forward(2, 1, 0)
        forward(2, 1, 1)
        relay(2, 1)
        forward(6, 2, 2)
        for j in range(REMOTE):
            o, k = offset_of(j), RANKS[j]

            @pl.when(s + 2 == SLOTS + j)
            def _():
                if k == 0:
                    (pass_copy(0) if o == HALF_WAY else z_copy(o)).wait_recv()
                    spread(j)
                elif k == 1 and o == 3:
                    for t in range(EXTRAS):
                        extra_copy(2, t).wait_recv()
                elif k == 1 and o == HALF_WAY:
                    for extra in range(1, EXTRAS):
                        pass_copy(extra).wait_recv()
                if k > 0:
                    pick(j)

        start_first(1, 2)
        start_first(3, 3)
        return carry

    lax.fori_loop(0, UNITS + 2, step, 0)

    for o in range(1, HALF_WAY):
        z_copy(o).wait_send()
    for hop in range(3):
        for t in range(EXTRAS):
            extra_copy(hop, t).wait_send()
    for k in range(SLOTS):
        relay_copy(k).wait_send()
        pass_copy(k).wait_send()

    def drain(j, carry):
        r_copy(j).wait_recv()
        y_copy(j).wait_send()
        c_copy(j).wait_send()
        d_copy(j).wait_send()
        r_copy(j).wait_send()
        return carry

    lax.fori_loop(0, REMOTE, drain, 0)

    def drain_sums(u, carry):
        p_copy(u).wait_send()
        h_copy(u).wait_send()
        return carry

    lax.fori_loop(0, UNITS, drain_sums, 0)

    for p in range(grad_x.shape[0] // BLOCK):
        unit = jnp.int32(0)
        for o in range(HOPS + 1):
            for k in range(SLOTS):
                here = k if o == 0 else SLOTS + UNIT_OF[o, k]
                unit = jnp.where((starts[o] + k == p) & (k < blocks[o]), here, unit)
        grad_x[pl.ds(p * BLOCK, BLOCK), :] = home[jnp.clip(unit, 0, UNITS - 1)]


def on_device(x_rows, grad_rows, w_gate_up, w_down, counts):
    rows, features = x_rows.shape
    units = w_down.shape[1]
    quarter = features // 4
    vmem = pl.BlockSpec(memory_space=pltpu.VMEM)
    held = pl.BlockSpec(memory_space=pl.ANY)
    b16, f32 = jnp.bfloat16, jnp.float32
    dma = pltpu.SemaphoreType.DMA
    grad_in, grad_out, grad_x = pl.pallas_call(
        lambda *refs: kernel(lax.axis_size("blk"), *refs),
        name="experts_backward",
        out_shape=(
            jax.ShapeDtypeStruct((2 * units, features), f32),
            jax.ShapeDtypeStruct((units, features), f32),
            jax.ShapeDtypeStruct((rows, quarter), b16),
        ),
        in_specs=[held, held, held, vmem, vmem],
        out_specs=(vmem, vmem, vmem),
        scratch_shapes=[
            pltpu.VMEM((rows // BLOCK, BLOCK, quarter), b16),
            pltpu.VMEM((rows // BLOCK, BLOCK, quarter), b16),
            pltpu.VMEM((FIRSTS + EXTRAS, 2, BLOCK, quarter), b16),
            pltpu.VMEM((SLOTS, 2, BLOCK, quarter), b16),
            *[pltpu.VMEM((EXTRAS, 2, BLOCK, quarter), b16)] * 3,
            pltpu.VMEM((EXTRAS - 1, 2, BLOCK, quarter), b16),
            pltpu.VMEM((UNITS, 2, BLOCK, features), b16),
            pltpu.VMEM((UNITS, 2, 2, BLOCK, quarter), b16),
            pltpu.VMEM((UNITS, 2, BLOCK, quarter), b16),
            pltpu.VMEM((UNITS, BLOCK, quarter), b16),
            pltpu.VMEM((UNITS, BLOCK, quarter), b16),
            pltpu.VMEM((REMOTE, BLOCK, quarter), b16),
            pltpu.VMEM((UNITS, BLOCK, quarter), b16),
            pltpu.SMEM(counts.shape[::-1], counts.dtype),
            dma((3 + 2 * SLOTS,)),
            *[dma((FIRSTS,))] * 2,
            *[dma((SLOTS,))] * 4,
            *[dma((3 * EXTRAS,))] * 2,
            *[dma((REMOTE,))] * 6,
            *[dma((UNITS,))] * 4,
            *[dma((REMOTE,))] * 2,
        ],
        compiler_params=pltpu.CompilerParams(
            collective_id=0, has_side_effects=True, vmem_limit_bytes=60 * 1024 * 1024
        ),
    )(
        counts.T,
        x_rows.reshape(-1, BLOCK, features),
        grad_rows.reshape(-1, BLOCK, features),
        w_gate_up.reshape(2 * units, features),
        w_down.reshape(units, features),
    )
    return (grad_in.reshape(1, 2, units, features), grad_out[None], grad_x)


def solution(mesh):
    finer = Mesh(mesh.devices.reshape(mesh.shape["blk"], 2, 2), ("blk", "dp_0", "dp_1"))
    placed = (P("blk", None), P("blk", None), P("blk", None, DP, None), P("blk", DP, None), P())
    return jax.shard_map(
        on_device,
        mesh=finer,
        in_specs=placed,
        out_specs=(P("blk", None, DP, None), P("blk", DP, None), P("blk", DP)),
        check_vma=False,
    )
```

```python
import jax
import jax.numpy as jnp
from jax import lax
from jax.experimental import pallas as pl
from jax.experimental.pallas import tpu as pltpu
from jax.sharding import Mesh
from jax.sharding import PartitionSpec as P

HOPS = 4
BLOCK = 128
SLOTS = 3
DP = ("dp_0", "dp_1")
MESH = pl.DeviceIdType.MESH
UNITS = SLOTS * (HOPS + 1)
REMOTE = SLOTS * HOPS


def contract_last(lhs, rhs):
    return lax.dot_general(lhs, rhs, (((1,), (1,)), ((), ())), preferred_element_type=jnp.float32)


def contract_first(lhs, rhs):
    return lax.dot_general(lhs, rhs, (((0,), (0,)), ((), ())), preferred_element_type=jnp.float32)


HALF_WAY = HOPS
COLUMN = 8
HALF = 32
FIRSTS = HOPS
EXTRAS = 3


def offset_of(j):
    def since(first):
        return (j + REMOTE - first) // REMOTE

    return 1 + 3 * since(1) - 3 * since(2) + since(4) + 2 * since(7) - since(9)


RANKS = (0, 0, 1, 2, 0, 1, 2, 1, 2, 0, 1, 2)
UNIT_OF = {(offset_of(j), RANKS[j]): j for j in range(REMOTE)}
FAR = UNIT_OF[HALF_WAY, 0]


def kernel(
    n_blk,
    counts_hbm,
    x_hbm,
    g_hbm,
    w_in,
    w_out,
    grad_in,
    grad_out,
    grad_x,
    x_quarter,
    g_quarter,
    staged,
    passing,
    past_1,
    past_2,
    past_3,
    past_4,
    full,
    pieces,
    pieces_in,
    half_out,
    half_in,
    home_out,
    home,
    counts,
    load_sem,
    z_send,
    z_recv,
    n_send,
    n_recv,
    m_send,
    m_recv,
    e_send,
    e_recv,
    y_send,
    y_recv,
    c_send,
    c_recv,
    d_send,
    d_recv,
    p_send,
    p_recv,
    h_send,
    h_recv,
    r_send,
    r_recv,
):
    b, y, c = lax.axis_index("blk"), lax.axis_index("dp_0"), lax.axis_index("dp_1")
    unit_count = w_out.shape[0]
    quarter = x_quarter.shape[2]

    def up(position, steps):
        level = lax.rem(position, COLUMN)
        return position - level + lax.rem(level + steps, COLUMN)

    def behind(position, o):
        crossed = 1 - (lax.rem(position, HALF) - o + HALF) // HALF
        return (lax.rem(position - o + n_blk, n_blk), y + crossed * (1 - 2 * y), c)

    def ahead(position, o):
        crossed = (lax.rem(position, HALF) + o) // HALF
        return (lax.rem(position + o, n_blk), y + crossed * (1 - 2 * y), c)

    y_peer, c_peer = (b, 1 - y, c), (b, y, 1 - c)
    relay_to = (up(b, 1), y, c)
    passed_to = behind(up(b, COLUMN - 1), HALF_WAY)

    def cols(y_of, c_of):
        return pl.ds(pl.multiple_of((2 * y_of + c_of) * quarter, quarter), quarter)

    own = cols(y, c)
    loads = []
    for held, source in ((x_quarter, x_hbm), (g_quarter, g_hbm)):
        loads.append(pltpu.make_async_copy(source.at[:, :, own], held, load_sem.at[len(loads)]))
    for k in range(SLOTS):
        for held, source in ((0, x_hbm), (1, g_hbm)):
            loads.append(pltpu.make_async_copy(source.at[k], full.at[k, held], load_sem.at[len(loads)]))
    loads.append(pltpu.make_async_copy(counts_hbm, counts, load_sem.at[len(loads)]))
    for load in loads:
        load.start()

    barrier = pltpu.get_barrier_semaphore()
    senders = [ahead(b, o) for o in range(1, HALF_WAY)] + [behind(b, o) for o in range(1, HOPS + 1)]
    home_of_far = ahead(b, HALF_WAY)
    senders += [(up(b, COLUMN - 1), y, c), (up(home_of_far[0], 1), home_of_far[1], c), y_peer, c_peer]
    for sender in senders:
        pl.semaphore_signal(barrier, 1, device_id=sender, device_id_type=MESH)

    for load in (*loads[:2], loads[-1]):
        load.wait()
    def split(position):
        live = [counts[o, position] for o in range(HOPS + 1)]
        blocks = [lax.shift_right_logical(n + (BLOCK - 1), 7) for n in live]
        starts, before = [jnp.int32(0)], [jnp.int32(0)]
        for o in range(HOPS):
            starts.append(starts[o] + blocks[o])
            before.append(before[o] + blocks[o] - 1)
        return live, blocks, starts, before

    live_of, blocks, starts, before = split(b)
    row_id = lax.broadcasted_iota(jnp.int32, (BLOCK, 1), 0)

    def remote(src, dst, send, recv, target):
        return pltpu.make_async_remote_copy(
            src_ref=src, dst_ref=dst, send_sem=send, recv_sem=recv, device_id=target, device_id_type=MESH
        )

    past = (past_1, past_2, past_3, past_4)

    def z_copy(o):
        part = full.at[SLOTS + UNIT_OF[o, 0], :, :, own]
        return remote(staged.at[o - 1], part, z_send.at[o - 1], z_recv.at[o - 1], behind(b, o))

    def extra_copy(hop, t):
        source = staged.at[FIRSTS + t] if hop == 0 else past[hop - 1].at[t]
        at = hop * EXTRAS + t
        return remote(source, past[hop].at[t], e_send.at[at], e_recv.at[at], behind(b, 1))

    def relay_copy(k):
        source = staged.at[HALF_WAY - 1 if k == 0 else FIRSTS + k]
        return remote(source, passing.at[k], n_send.at[k], n_recv.at[k], relay_to)

    def pass_copy(k):
        part = full.at[SLOTS + FAR, :, :, own] if k == 0 else past_4.at[k - 1]
        landed = z_recv.at[HALF_WAY - 1] if k == 0 else m_recv.at[k]
        return remote(passing.at[k], part, m_send.at[k], landed, passed_to)

    def place(slot, block):
        block = jnp.clip(block, 0, x_quarter.shape[0] - 1)
        staged[slot, 0] = x_quarter[block]
        return g_quarter[block]

    zero = jnp.zeros((), jnp.bfloat16)
    def place_first(o):
        staged[o - 1, 1] = jnp.where(row_id < live_of[o], place(o - 1, starts[o]), zero)

    place_first(1)
    pl.semaphore_wait(barrier, len(senders))
    z_copy(1).start()
    place_first(HALF_WAY)
    relay_copy(0).start()
    for t in range(EXTRAS):
        block = jnp.int32(0)
        for o in range(HOPS + 1):
            at = t - before[o]
            block = jnp.where((at >= 0) & (at < blocks[o] - 1), starts[o] + 1 + at, block)
        staged[FIRSTS + t, 1] = place(FIRSTS + t, block)
        extra_copy(0, t).start()
    place_first(2)
    place_first(3)

    for load in loads[2:-1]:
        load.wait()
    for k in range(SLOTS):
        live = row_id < live_of[0] - k * BLOCK
        full[k, 1] = jnp.where(live, full[k, 1], jnp.zeros((), jnp.bfloat16))
    grad_in[...] = jnp.zeros_like(grad_in)
    grad_out[...] = jnp.zeros_like(grad_out)

    def y_copy(j):
        part = full.at[SLOTS + j, :, :, cols(ahead(b, offset_of(j))[1], c)]
        return remote(part, part, y_send.at[j], y_recv.at[j], y_peer)

    def c_copy(j):
        part = full.at[SLOTS + j, :, :, cols(ahead(b, offset_of(j))[1], c)]
        return remote(part, part, c_send.at[j], c_recv.at[j], c_peer)

    def d_copy(j):
        part = full.at[SLOTS + j, :, :, cols(1 - ahead(b, offset_of(j))[1], c)]
        return remote(part, part, d_send.at[j], d_recv.at[j], c_peer)

    def spread(j):
        y_copy(j).start()
        c_copy(j).start()

    def pick(j):
        o, k = offset_of(j), RANKS[j]
        home_of, y_of, _ = ahead(b, o)
        live, _, _, first = split(home_of)
        lowest = 1 if o == HALF_WAY else 0
        t = jnp.clip(first[o] + k - 1, lowest, EXTRAS - 1) - lowest
        part = cols(y_of, c)
        full[SLOTS + j, 0, :, part] = past[o - 1][t, 0]
        full[SLOTS + j, 1, :, part] = jnp.where(row_id < live[o] - k * BLOCK, past[o - 1][t, 1], zero)
        spread(j)

    def p_copy(u):
        return remote(pieces.at[u, 1 - c], pieces_in.at[u], p_send.at[u], p_recv.at[u], c_peer)

    def h_copy(u):
        return remote(half_out.at[u], half_in.at[u], h_send.at[u], h_recv.at[u], y_peer)

    def r_copy(j):
        return remote(home_out.at[j], home.at[SLOTS + j], r_send.at[j], r_recv.at[j], ahead(b, offset_of(j)))

    def finished_by(u):
        away = (u + UNITS - SLOTS) // UNITS
        return ahead(b, away * offset_of(u - away * SLOTS))[1]

    def compute(u):
        rows_in, rows_cot = full[u, 0], full[u, 1]
        projected = contract_last(rows_in, w_in[...])
        gate_pre, up_pre = projected[:, :unit_count], projected[:, unit_count:]
        sigmoid_gate = jax.nn.sigmoid(gate_pre)
        active = gate_pre * sigmoid_gate
        hidden = (active * up_pre).astype(jnp.bfloat16)
        hidden_grad = contract_last(rows_cot, w_out[...])
        gate_grad = hidden_grad * up_pre * sigmoid_gate * (1.0 + gate_pre * (1.0 - sigmoid_gate))
        both = jnp.concatenate([gate_grad, hidden_grad * active], axis=1).astype(jnp.bfloat16)
        for q in range(4):
            pieces[u, q % 2, q // 2] = jnp.dot(
                both, w_in[:, q * quarter : (q + 1) * quarter], preferred_element_type=jnp.float32
            ).astype(jnp.bfloat16)
        p_copy(u).start()
        grad_in[...] += contract_first(both, rows_in)
        grad_out[...] += contract_first(hidden, rows_cot)

    def partial_sum(u, y_of):
        return pieces[u, c, y_of].astype(jnp.float32) + pieces_in[u, y_of].astype(jnp.float32)

    def step(s, carry):
        def forward(at, hop, t):
            @pl.when(s == at)
            def _():
                extra_copy(hop - 1, t).wait_recv()
                extra_copy(hop, t).start()

        def relay(at, k):
            @pl.when(s == at)
            def _():
                relay_copy(k).wait_recv()
                pass_copy(k).start()
                if k == 0:
                    relay_copy(1).start()
                    relay_copy(2).start()

        def start_first(at, o):
            @pl.when(s == at)
            def _():
                z_copy(o).start()

        @pl.when(s >= 2)
        def _():
            u = s - 2
            h_copy(u).wait_recv()
            total = (partial_sum(u, finished_by(u)) + half_in[u].astype(jnp.float32)).astype(jnp.bfloat16)

            @pl.when(u < SLOTS)
            def _():
                home[u] = total

            @pl.when(u >= SLOTS)
            def _():
                home_out[u - SLOTS] = total
                r_copy(u - SLOTS).start()

        @pl.when((s >= 1) & (s < UNITS + 1))
        def _():
            u = s - 1
            p_copy(u).wait_recv()
            half_out[u] = partial_sum(u, 1 - finished_by(u)).astype(jnp.bfloat16)
            h_copy(u).start()

        @pl.when(s < UNITS)
        def _():
            @pl.when(s >= SLOTS)
            def _():
                c_copy(s - SLOTS).wait_recv()
                d_copy(s - SLOTS).wait_recv()

            compute(s)

        forward(2, 1, 2)
        relay(2, 2)
        forward(4, 2, 0)
        forward(5, 2, 1)

        @pl.when((s + 1 >= SLOTS) & (s + 1 < UNITS))
        def _():
            j = s + 1 - SLOTS
            y_copy(j).wait_recv()
            d_copy(j).start()

        relay(0, 0)
        forward(1, 1, 0)
        forward(1, 1, 1)
        relay(1, 1)
        forward(5, 2, 2)
        for j in range(REMOTE):
            o, k = offset_of(j), RANKS[j]

            @pl.when(s + 3 == SLOTS + j)
            def _():
                if k == 0:
                    (pass_copy(0) if o == HALF_WAY else z_copy(o)).wait_recv()
                    spread(j)
                elif k == 1 and o == 3:
                    for t in range(EXTRAS):
                        extra_copy(2, t).wait_recv()
                elif k == 1 and o == HALF_WAY:
                    for extra in range(1, EXTRAS):
                        pass_copy(extra).wait_recv()
                if k > 0:
                    pick(j)

        start_first(0, 2)
        start_first(2, 3)
        return carry

    lax.fori_loop(0, UNITS + 2, step, 0)

    for o in range(1, HALF_WAY):
        z_copy(o).wait_send()
    for hop in range(3):
        for t in range(EXTRAS):
            extra_copy(hop, t).wait_send()
    for k in range(SLOTS):
        relay_copy(k).wait_send()
        pass_copy(k).wait_send()

    def drain(j, carry):
        r_copy(j).wait_recv()
        y_copy(j).wait_send()
        c_copy(j).wait_send()
        d_copy(j).wait_send()
        r_copy(j).wait_send()
        return carry

    lax.fori_loop(0, REMOTE, drain, 0)

    def drain_sums(u, carry):
        p_copy(u).wait_send()
        h_copy(u).wait_send()
        return carry

    lax.fori_loop(0, UNITS, drain_sums, 0)

    for p in range(grad_x.shape[0] // BLOCK):
        unit = jnp.int32(0)
        for o in range(HOPS + 1):
            for k in range(SLOTS):
                here = k if o == 0 else SLOTS + UNIT_OF[o, k]
                unit = jnp.where((starts[o] + k == p) & (k < blocks[o]), here, unit)
        grad_x[pl.ds(p * BLOCK, BLOCK), :] = home[jnp.clip(unit, 0, UNITS - 1)]


def on_device(x_rows, grad_rows, w_gate_up, w_down, counts):
    rows, features = x_rows.shape
    units = w_down.shape[1]
    quarter = features // 4
    vmem = pl.BlockSpec(memory_space=pltpu.VMEM)
    held = pl.BlockSpec(memory_space=pl.ANY)
    b16, f32 = jnp.bfloat16, jnp.float32
    dma = pltpu.SemaphoreType.DMA
    grad_in, grad_out, grad_x = pl.pallas_call(
        lambda *refs: kernel(lax.axis_size("blk"), *refs),
        name="experts_backward",
        out_shape=(
            jax.ShapeDtypeStruct((2 * units, features), f32),
            jax.ShapeDtypeStruct((units, features), f32),
            jax.ShapeDtypeStruct((rows, quarter), b16),
        ),
        in_specs=[held, held, held, vmem, vmem],
        out_specs=(vmem, vmem, vmem),
        scratch_shapes=[
            pltpu.VMEM((rows // BLOCK, BLOCK, quarter), b16),
            pltpu.VMEM((rows // BLOCK, BLOCK, quarter), b16),
            pltpu.VMEM((FIRSTS + EXTRAS, 2, BLOCK, quarter), b16),
            pltpu.VMEM((SLOTS, 2, BLOCK, quarter), b16),
            *[pltpu.VMEM((EXTRAS, 2, BLOCK, quarter), b16)] * 3,
            pltpu.VMEM((EXTRAS - 1, 2, BLOCK, quarter), b16),
            pltpu.VMEM((UNITS, 2, BLOCK, features), b16),
            pltpu.VMEM((UNITS, 2, 2, BLOCK, quarter), b16),
            pltpu.VMEM((UNITS, 2, BLOCK, quarter), b16),
            pltpu.VMEM((UNITS, BLOCK, quarter), b16),
            pltpu.VMEM((UNITS, BLOCK, quarter), b16),
            pltpu.VMEM((REMOTE, BLOCK, quarter), b16),
            pltpu.VMEM((UNITS, BLOCK, quarter), b16),
            pltpu.SMEM(counts.shape[::-1], counts.dtype),
            dma((3 + 2 * SLOTS,)),
            *[dma((FIRSTS,))] * 2,
            *[dma((SLOTS,))] * 4,
            *[dma((3 * EXTRAS,))] * 2,
            *[dma((REMOTE,))] * 6,
            *[dma((UNITS,))] * 4,
            *[dma((REMOTE,))] * 2,
        ],
        compiler_params=pltpu.CompilerParams(
            collective_id=0, has_side_effects=True, vmem_limit_bytes=60 * 1024 * 1024
        ),
    )(
        counts.T,
        x_rows.reshape(-1, BLOCK, features),
        grad_rows.reshape(-1, BLOCK, features),
        w_gate_up.reshape(2 * units, features),
        w_down.reshape(units, features),
    )
    return (grad_in.reshape(1, 2, units, features), grad_out[None], grad_x)


def solution(mesh):
    finer = Mesh(mesh.devices.reshape(mesh.shape["blk"], 2, 2), ("blk", "dp_0", "dp_1"))
    placed = (P("blk", None), P("blk", None), P("blk", None, DP, None), P("blk", DP, None), P())
    return jax.shard_map(
        on_device,
        mesh=finer,
        in_specs=placed,
        out_specs=(P("blk", None, DP, None), P("blk", DP, None), P("blk", DP)),
        check_vma=False,
    )
```

```python
import jax
import jax.numpy as jnp
from jax import lax
from jax.experimental import pallas as pl
from jax.experimental.pallas import tpu as pltpu
from jax.sharding import Mesh
from jax.sharding import PartitionSpec as P

HOPS = 4
BLOCK = 128
SLOTS = 3
DP = ("dp_0", "dp_1")
MESH = pl.DeviceIdType.MESH
UNITS = SLOTS * (HOPS + 1)
REMOTE = SLOTS * HOPS


def contract_last(lhs, rhs):
    return lax.dot_general(lhs, rhs, (((1,), (1,)), ((), ())), preferred_element_type=jnp.float32)


def contract_first(lhs, rhs):
    return lax.dot_general(lhs, rhs, (((0,), (0,)), ((), ())), preferred_element_type=jnp.float32)


HALF_WAY = HOPS
COLUMN = 8
HALF = 32
IN_FLIGHT = 3


def offset_of(j):
    turn, i = j // HOPS, j % HOPS
    last = turn // (SLOTS - 1)
    return (1 - last) * (i + 1 + i // 2 - 2 * (i // 3)) + last * (HOPS - i)


UNIT_OF = {(offset_of(j), j // HOPS): j for j in range(REMOTE)}
DIRECT = [j for j in range(REMOTE) if offset_of(j) < HALF_WAY]
RELAYED = [j for j in range(REMOTE) if offset_of(j) == HALF_WAY]


def kernel(
    n_blk,
    counts_hbm,
    x_hbm,
    g_hbm,
    w_in,
    w_out,
    grad_in_hbm,
    grad_out_hbm,
    grad_x,
    grad_in,
    grad_out,
    both_of,
    hidden_of,
    store_sem,
    x_quarter,
    g_quarter,
    staged,
    passing,
    full,
    pieces,
    pieces_in,
    half_out,
    half_in,
    home_out,
    home,
    counts,
    load_sem,
    z_send,
    z_recv,
    n_send,
    n_recv,
    y_send,
    y_recv,
    c_send,
    c_recv,
    d_send,
    d_recv,
    p_send,
    p_recv,
    h_send,
    h_recv,
    r_send,
    r_recv,
):
    b, y, c = lax.axis_index("blk"), lax.axis_index("dp_0"), lax.axis_index("dp_1")
    unit_count = w_out.shape[0]
    quarter = x_quarter.shape[3]

    def up(position, steps):
        level = lax.rem(position, COLUMN)
        return position - level + lax.rem(level + steps, COLUMN)

    def behind(position, o):
        crossed = 1 - (lax.rem(position, HALF) - o + HALF) // HALF
        return (lax.rem(position - o + n_blk, n_blk), y + crossed * (1 - 2 * y), c)

    def ahead(position, o):
        crossed = (lax.rem(position, HALF) + o) // HALF
        return (lax.rem(position + o, n_blk), y + crossed * (1 - 2 * y), c)

    y_peer, c_peer = (b, 1 - y, c), (b, y, 1 - c)
    relay_to = (up(b, 1), y, c)
    passed_to = behind(up(b, COLUMN - 1), HALF_WAY)

    def cols(y_of, c_of):
        return pl.ds(pl.multiple_of((2 * y_of + c_of) * quarter, quarter), quarter)

    own = cols(y, c)
    loads = []
    for y_of in range(2):
        for held, source in ((x_quarter, x_hbm), (g_quarter, g_hbm)):
            copy = pltpu.make_async_copy(source.at[:, :, cols(y_of, c)], held.at[y_of], load_sem.at[len(loads)])
            loads.append(copy)
    for k in range(SLOTS):
        for held, source in ((0, x_hbm), (1, g_hbm)):
            loads.append(pltpu.make_async_copy(source.at[k], full.at[k, held], load_sem.at[len(loads)]))
    loads.append(pltpu.make_async_copy(counts_hbm, counts, load_sem.at[len(loads)]))
    for load in loads:
        load.start()

    barrier = pltpu.get_barrier_semaphore()
    senders = [ahead(b, o) for o in range(1, HALF_WAY)] + [behind(b, o) for o in range(1, HOPS + 1)]
    home_of_far = ahead(b, HALF_WAY)
    senders += [(up(b, COLUMN - 1), y, c), (up(home_of_far[0], 1), home_of_far[1], c), y_peer, c_peer]
    for sender in senders:
        pl.semaphore_signal(barrier, 1, device_id=sender, device_id_type=MESH)

    for load in (*loads[:4], loads[-1]):
        load.wait()
    live_of = [counts[o, b] for o in range(HOPS + 1)]
    blocks = [lax.shift_right_logical(n + (BLOCK - 1), 7) for n in live_of]
    starts = [jnp.int32(0)]
    for o in range(HOPS):
        starts.append(starts[o] + blocks[o])
    row_id = lax.broadcasted_iota(jnp.int32, (BLOCK, 1), 0)

    def remote(src, dst, send, recv, target):
        return pltpu.make_async_remote_copy(
            src_ref=src, dst_ref=dst, send_sem=send, recv_sem=recv, device_id=target, device_id_type=MESH
        )

    def z_copy(j, target):
        part = full.at[SLOTS + j, :, :, cols(target[1], c)]
        return remote(staged.at[j], part, z_send.at[j], z_recv.at[j], target)

    def start_direct(j):
        z_copy(j, behind(b, offset_of(j))).start()

    def relay_copy(k):
        j = UNIT_OF[HALF_WAY, k]
        return remote(staged.at[j], passing.at[k], z_send.at[j], n_recv.at[k], relay_to)

    def pass_copy(k):
        j = UNIT_OF[HALF_WAY, k]
        part = full.at[SLOTS + j, :, :, cols(passed_to[1], c)]
        return remote(passing.at[k], part, n_send.at[k], z_recv.at[j], passed_to)

    for count, j in enumerate(RELAYED[:1] + DIRECT[:1] + RELAYED[1:] + DIRECT[1:]):
        k, o = j // HOPS, offset_of(j)
        block = jnp.clip(starts[o] + jnp.minimum(k, blocks[o] - 1), 0, x_quarter.shape[1] - 1)
        y_of = behind(b, o)[1]
        staged[j, 0] = x_quarter[y_of, block]
        live = row_id < live_of[o] - k * BLOCK
        staged[j, 1] = jnp.where(live, g_quarter[y_of, block], jnp.zeros((), jnp.bfloat16))
        if count == 0:
            pl.semaphore_wait(barrier, len(senders))
        if o == HALF_WAY:
            relay_copy(k).start()
        elif j in DIRECT[:IN_FLIGHT]:
            start_direct(j)

    for load in loads[4:-1]:
        load.wait()
    for k in range(SLOTS):
        live = row_id < live_of[0] - k * BLOCK
        full[k, 1] = jnp.where(live, full[k, 1], jnp.zeros((), jnp.bfloat16))
    grad_in[...] = jnp.zeros_like(grad_in)
    grad_out[...] = jnp.zeros_like(grad_out)

    def y_copy(j):
        part = full.at[SLOTS + j, :, :, own]
        return remote(part, part, y_send.at[j], y_recv.at[j], y_peer)

    def c_copy(j):
        part = full.at[SLOTS + j, :, :, own]
        return remote(part, part, c_send.at[j], c_recv.at[j], c_peer)

    def d_copy(j):
        part = full.at[SLOTS + j, :, :, cols(1 - y, c)]
        return remote(part, part, d_send.at[j], d_recv.at[j], c_peer)

    def p_copy(u):
        return remote(pieces.at[u, 1 - c], pieces_in.at[u], p_send.at[u], p_recv.at[u], c_peer)

    def h_copy(u):
        return remote(half_out.at[u], half_in.at[u], h_send.at[u], h_recv.at[u], y_peer)

    def r_copy(j):
        return remote(home_out.at[j], home.at[SLOTS + j], r_send.at[j], r_recv.at[j], ahead(b, offset_of(j)))

    def finished_by(u):
        away = (u + UNITS - SLOTS) // UNITS
        return ahead(b, away * offset_of(u - away * SLOTS))[1]

    def compute(u):
        rows_in, rows_cot = full[u, 0], full[u, 1]
        projected = contract_last(rows_in, w_in[...])
        gate_pre, up_pre = projected[:, :unit_count], projected[:, unit_count:]
        sigmoid_gate = jax.nn.sigmoid(gate_pre)
        active = gate_pre * sigmoid_gate
        hidden = (active * up_pre).astype(jnp.bfloat16)
        hidden_grad = contract_last(rows_cot, w_out[...])
        gate_grad = hidden_grad * up_pre * sigmoid_gate * (1.0 + gate_pre * (1.0 - sigmoid_gate))
        both = jnp.concatenate([gate_grad, hidden_grad * active], axis=1).astype(jnp.bfloat16)
        for q in range(4):
            pieces[u, q % 2, q // 2] = jnp.dot(
                both, w_in[:, q * quarter : (q + 1) * quarter], preferred_element_type=jnp.float32
            ).astype(jnp.bfloat16)
        p_copy(u).start()
        both_of[...] = both
        hidden_of[...] = hidden

    def add_grads(u):
        grad_in[...] += contract_first(both_of[...], full[u, 0])
        grad_out[...] += contract_first(hidden_of[...], full[u, 1])

    def partial_sum(u, y_of):
        return pieces[u, c, y_of].astype(jnp.float32) + pieces_in[u, y_of].astype(jnp.float32)

    def finished(u):
        h_copy(u).wait_recv()
        return (partial_sum(u, finished_by(u)) + half_in[u].astype(jnp.float32)).astype(jnp.bfloat16)

    def send_home(j, total):
        home_out[j] = total
        r_copy(j).start()

    def step(s, carry):
        for i, j in enumerate(DIRECT[IN_FLIGHT:]):

            @pl.when(s == i + 2)
            def _():
                z_copy(DIRECT[i], y_peer).wait_send()
                start_direct(j)

        @pl.when(s >= 2)
        def _():
            u = s - 2
            total = finished(u)

            @pl.when(u < SLOTS)
            def _():
                home[u] = total

            @pl.when(u >= SLOTS)
            def _():
                send_home(u - SLOTS, total)

        @pl.when((s >= 1) & (s < UNITS + 1))
        def _():
            u = s - 1
            p_copy(u).wait_recv()
            half_out[u] = partial_sum(u, 1 - finished_by(u)).astype(jnp.bfloat16)
            h_copy(u).start()
            add_grads(u)

        @pl.when(s < UNITS)
        def _():
            @pl.when(s >= SLOTS)
            def _():
                c_copy(s - SLOTS).wait_recv()
                d_copy(s - SLOTS).wait_recv()

            compute(s)

        @pl.when((s + 1 >= SLOTS) & (s + 1 < UNITS))
        def _():
            j = s + 1 - SLOTS
            y_copy(j).wait_recv()
            d_copy(j).start()

        for k in range(SLOTS):

            @pl.when(s == k)
            def _():
                relay_copy(k).wait_recv()
                pass_copy(k).start()

        @pl.when((s + 2 >= SLOTS) & (s + 2 < UNITS))
        def _():
            j = s + 2 - SLOTS
            z_copy(j, y_peer).wait_recv()
            y_copy(j).start()
            c_copy(j).start()

        return carry

    lax.fori_loop(0, UNITS + 1, step, 0)
    stores = [
        pltpu.make_async_copy(grad_in, grad_in_hbm, store_sem.at[0]),
        pltpu.make_async_copy(grad_out, grad_out_hbm, store_sem.at[1]),
    ]
    for store in stores:
        store.start()
    send_home(REMOTE - 1, finished(UNITS - 1))

    for j in RELAYED + DIRECT[-IN_FLIGHT:]:
        z_copy(j, y_peer).wait_send()
    for k in range(SLOTS):
        pass_copy(k).wait_send()

    def drain(j, carry):
        r_copy(j).wait_recv()
        y_copy(j).wait_send()
        c_copy(j).wait_send()
        d_copy(j).wait_send()
        r_copy(j).wait_send()
        return carry

    lax.fori_loop(0, REMOTE, drain, 0)

    def drain_sums(u, carry):
        p_copy(u).wait_send()
        h_copy(u).wait_send()
        return carry

    lax.fori_loop(0, UNITS, drain_sums, 0)
    for store in stores:
        store.wait()

    for p in range(grad_x.shape[0] // BLOCK):
        unit = jnp.int32(0)
        for o in range(HOPS + 1):
            for k in range(SLOTS):
                here = k if o == 0 else SLOTS + UNIT_OF[o, k]
                unit = jnp.where((starts[o] + k == p) & (k < blocks[o]), here, unit)
        grad_x[pl.ds(p * BLOCK, BLOCK), :] = home[jnp.clip(unit, 0, UNITS - 1)]


def on_device(x_rows, grad_rows, w_gate_up, w_down, counts):
    rows, features = x_rows.shape
    units = w_down.shape[1]
    quarter = features // 4
    vmem = pl.BlockSpec(memory_space=pltpu.VMEM)
    held = pl.BlockSpec(memory_space=pl.ANY)
    b16, f32 = jnp.bfloat16, jnp.float32
    dma = pltpu.SemaphoreType.DMA
    grad_in, grad_out, grad_x = pl.pallas_call(
        lambda *refs: kernel(lax.axis_size("blk"), *refs),
        name="experts_backward",
        out_shape=(
            jax.ShapeDtypeStruct((2 * units, features), f32),
            jax.ShapeDtypeStruct((units, features), f32),
            jax.ShapeDtypeStruct((rows, quarter), b16),
        ),
        in_specs=[held, held, held, vmem, vmem],
        out_specs=(held, held, vmem),
        scratch_shapes=[
            pltpu.VMEM((2 * units, features), f32),
            pltpu.VMEM((units, features), f32),
            pltpu.VMEM((BLOCK, 2 * units), b16),
            pltpu.VMEM((BLOCK, units), b16),
            dma((2,)),
            pltpu.VMEM((2, rows // BLOCK, BLOCK, quarter), b16),
            pltpu.VMEM((2, rows // BLOCK, BLOCK, quarter), b16),
            pltpu.VMEM((REMOTE, 2, BLOCK, quarter), b16),
            pltpu.VMEM((SLOTS, 2, BLOCK, quarter), b16),
            pltpu.VMEM((UNITS, 2, BLOCK, features), b16),
            pltpu.VMEM((UNITS, 2, 2, BLOCK, quarter), b16),
            pltpu.VMEM((UNITS, 2, BLOCK, quarter), b16),
            pltpu.VMEM((UNITS, BLOCK, quarter), b16),
            pltpu.VMEM((UNITS, BLOCK, quarter), b16),
            pltpu.VMEM((REMOTE, BLOCK, quarter), b16),
            pltpu.VMEM((UNITS, BLOCK, quarter), b16),
            pltpu.SMEM(counts.shape[::-1], counts.dtype),
            dma((5 + 2 * SLOTS,)),
            *[dma((REMOTE,))] * 2,
            *[dma((SLOTS,))] * 2,
            *[dma((REMOTE,))] * 6,
            *[dma((UNITS,))] * 4,
            *[dma((REMOTE,))] * 2,
        ],
        compiler_params=pltpu.CompilerParams(
            collective_id=0, has_side_effects=True, vmem_limit_bytes=60 * 1024 * 1024
        ),
    )(
        counts.T,
        x_rows.reshape(-1, BLOCK, features),
        grad_rows.reshape(-1, BLOCK, features),
        w_gate_up.reshape(2 * units, features),
        w_down.reshape(units, features),
    )
    return (grad_in.reshape(1, 2, units, features), grad_out[None], grad_x)


def solution(mesh):
    finer = Mesh(mesh.devices.reshape(mesh.shape["blk"], 2, 2), ("blk", "dp_0", "dp_1"))
    placed = (P("blk", None), P("blk", None), P("blk", None, DP, None), P("blk", DP, None), P())
    return jax.shard_map(
        on_device,
        mesh=finer,
        in_specs=placed,
        out_specs=(P("blk", None, DP, None), P("blk", DP, None), P("blk", DP)),
        check_vma=False,
    )
```
